512 devices in a mesh: clip: 64 (over z, y_lo, core), disc: 8 (over y_hi, x).
Axes of the slice: x: 4, y: 4 (y_hi: 2, y_lo: 2; y = y_hi * 2 + y_lo), z: 16, core: 2. Of those that a mesh axis runs over, the one named last changes fastest.
Arguments:
- waveform: bfloat16 [64, 2, 32768], P('clip', None, 'disc'), may hold values from -3 to 3
- window_length: int32 [8], P('disc'), may hold values from 256 to 1024
- first_weight: bfloat16 [8, 1024, 512], P('disc'), may hold values from -0.1875 to 0.1875
- first_bias: float32 [8, 512], P('disc'), may hold values from -2 to 2
- head_weight: bfloat16 [8, 512], P('disc'), may hold values from -0.25 to 0.25
Outputs:
- waveform_grad: float32 [64, 2, 32768], P('clip', None, 'disc')
- first_grad: float32 [8, 1024, 512], P('disc', 'clip')
- head_grad: float32 [8, 512, 2], P('disc', 'clip')
The draws below stay inside these ranges and needn't reach their ends.
Inputs may be any that keep to these rules, and one draw needn't show every extreme that they name: `window_length`: each branch's window length in samples, centred in a frame of 1024.
All inputs are finite; a program needn't handle non-finite values.
Results may differ from the reference program's by a relative error of at most 0.04.
Values may be sent and summed in bfloat16 or wider, within the bound.
A program may use at most 64 MiB of HBM per device.

```python
import math
import jax
import jax.numpy as jnp
from jax import lax

FR = 1024
HID = 512
BRANCHES = 8
SEG = 32768
CLIPS = 64


def plant(entries, rng, low, high):
    place = [jax.random.randint(jax.random.fold_in(rng, axis), (), 0, length) for axis, length in enumerate(entries.shape)]
    main_axis = entries.shape.index(max(entries.shape))
    neighbour = place[:main_axis] + [(place[main_axis] + 1) % entries.shape[main_axis]] + place[main_axis + 1:]
    return entries.at[tuple(place)].set(low).at[tuple(neighbour)].set(high)


def steps_of(stream_key, extent, cuts, least, high):
    gain, own = 1.0, jax.random.fold_in(stream_key, 6)
    for axis_at, shards_of in cuts:
        steps = jnp.exp(jax.random.uniform(jax.random.fold_in(own, axis_at), (shards_of,), jnp.float32, least / len(cuts), high / len(cuts)))
        gain = gain * jnp.repeat(steps, extent[axis_at] // shards_of).reshape([-1 if axis == axis_at else 1 for axis in range(len(extent))])
    return gain


def scatter_about(rng, shape, spread, bound, split=(), held_as=jnp.bfloat16):
    level = steps_of(rng, shape, split, -0.22, 0.18) if split else 1.0
    result = jax.random.normal(rng, shape, jnp.float32) * spread * level
    return jnp.minimum(jnp.maximum(result, -bound), bound).astype(held_as)


def setup_inputs(seed: int = 0) -> dict:
    keys = jax.random.split(jax.random.key(seed), 6)
    waveform = scatter_about(keys[0], (CLIPS, 2, SEG), 0.5, 3.0, ((0, 64), (2, 8)))
    window_length = plant(jax.random.randint(keys[1], (BRANCHES,), FR // 4, FR + 1), jax.random.fold_in(keys[1], 1), FR // 4, FR).astype(jnp.int32)
    first_weight = scatter_about(keys[2], (BRANCHES, FR, HID), FR ** -0.5, 0.1875, ((0, 8),))
    first_bias = scatter_about(keys[3], (BRANCHES, HID), 0.3, 2.0, ((0, 8),), jnp.float32)
    head_weight = scatter_about(keys[4], (BRANCHES, HID), HID ** -0.5, 0.25, ((0, 8),))
    return dict(waveform=waveform, window_length=window_length, first_weight=first_weight, first_bias=first_bias, head_weight=head_weight)


GEN_WEIGHT = 10.0
LEAK = 0.2

def make_table(length, frame):
    positions = jnp.arange(frame, dtype=jnp.int32)
    shifted = positions - (frame - length) // 2
    inside = (shifted >= 0) & (shifted < length)
    phases = 2.0 * jnp.pi * shifted.astype(jnp.float32) / length.astype(jnp.float32)
    window = jnp.where(inside, 0.5 - 0.5 * jnp.cos(phases), 0.0)
    column = jnp.arange(frame // 2, dtype=jnp.int32)
    angles = 2.0 * jnp.pi * (positions[:, None] * column[None, :] % frame).astype(jnp.float32) / frame
    factor = window[:, None] / math.sqrt(frame)
    return jnp.concatenate([jnp.cos(angles) * factor, -jnp.sin(angles) * factor], axis=1).astype(jnp.bfloat16)

def make_frames(signal, hop_size):
    length = signal.shape[-1]
    frame_count = length // hop_size
    leading = signal.shape[:-1]
    padded = jnp.pad(signal, [(0, 0)] * len(leading) + [(2 * hop_size, hop_size)])
    blocks = padded.reshape(leading + (frame_count + 3, hop_size))
    return jnp.concatenate([blocks[..., offset:offset + frame_count, :] for offset in range(4)], axis=-1)

def intersection_add(frame_delta, hop_size):
    frame_count = frame_delta.shape[-2]
    leading = frame_delta.shape[:-2]
    pieces = frame_delta.reshape(leading + (frame_count, 4, hop_size))
    summed = jnp.zeros(leading + (frame_count + 3, hop_size), jnp.float32)
    for offset in range(4):
        padding = [(0, 0)] * len(leading) + [(offset, 3 - offset), (0, 0)]
        summed = summed + jnp.pad(pieces[..., offset, :], padding)
    return summed[..., 2:frame_count + 2, :].reshape(leading + (frame_count * hop_size,))

def forward_part(rows, table, weight, bias, head):
    spectrum = jnp.dot(rows, table, preferred_element_type=jnp.float32).astype(jnp.bfloat16)
    preact = jnp.dot(spectrum, weight, preferred_element_type=jnp.float32) + bias[None, :]
    slopes = jnp.where(preact > 0, 1.0, LEAK)
    hidden = (preact * slopes).astype(jnp.bfloat16)
    logits = jnp.dot(hidden, head, preferred_element_type=jnp.float32)
    head_wide = head.astype(jnp.float32)[None, :]
    disc_delta = (logits[:, None] * head_wide * slopes).astype(jnp.bfloat16)
    gen_delta = (GEN_WEIGHT * (logits - 1.0)[:, None] * head_wide * slopes).astype(jnp.bfloat16)
    head_terms = jnp.stack([lax.optimization_barrier(jnp.sum(logits[:, None] * hidden.astype(jnp.float32), axis=0)), lax.optimization_barrier(jnp.sum(disc_delta.astype(jnp.float32), axis=0))], axis=1)
    return (spectrum, disc_delta, gen_delta, head_terms)

def weight_product(spectrum, disc_delta):
    return lax.dot_general(spectrum, disc_delta, (((0,), (0,)), ((), ())), preferred_element_type=jnp.float32)

def generator_back(gen_delta, weight, table):
    spec_delta = jnp.dot(gen_delta, weight.T, preferred_element_type=jnp.float32).astype(jnp.bfloat16)
    return jnp.dot(spec_delta, table.T, preferred_element_type=jnp.float32)

def reference(waveform, window_length, first_weight, first_bias, head_weight):
    frame = first_weight.shape[1]
    hop_size = frame // 4
    rows = make_frames(waveform, hop_size).reshape(-1, frame)

    def branch_step(summed, inputs):
        length, weight, bias, head = inputs
        table = make_table(length, frame)
        spectrum, disc_delta, gen_delta, head_terms = forward_part(rows, table, weight, bias, head)
        weight_grad = weight_product(spectrum, disc_delta)
        frame_delta = generator_back(gen_delta, weight, table)
        frame_delta = frame_delta.reshape(waveform.shape[:2] + (-1, frame))
        summed = summed + intersection_add(frame_delta, hop_size)
        return (summed, (weight_grad, head_terms))
    start_sum = jnp.zeros(waveform.shape, jnp.float32)
    summed, outputs = lax.scan(branch_step, start_sum, (window_length, first_weight, first_bias, head_weight))
    return (summed, outputs[0], outputs[1])
```

```python
import math

import jax
import jax.numpy as jnp
import numpy as np
from jax import lax
from jax.experimental import pallas as pl
from jax.experimental.pallas import tpu as pltpu
from jax.sharding import PartitionSpec as P

GEN_WEIGHT = 10.0
LEAK = 0.2
MESH = pl.DeviceIdType.MESH
GROUP = 16
X_SIZE = 4
Z_SIZE = 16
F32 = jnp.float32
BF16 = jnp.bfloat16


def twiddles(frame):
    column = np.arange(frame // 2)
    coarse = (np.arange(0, frame, GROUP)[:, None] * column[None, :]) % frame
    fine = (np.arange(GROUP)[:, None] * column[None, :]) % frame
    angle = 2.0 * np.pi / frame
    coarse = np.concatenate([np.cos(coarse * angle), np.sin(coarse * angle)], axis=0)
    fine = np.concatenate([np.cos(fine * angle), np.sin(fine * angle)], axis=0)
    return coarse[:, None, :].astype(np.float32), fine.astype(np.float32)


def remote(src, dst, send_sem, recv_sem, device):
    return pltpu.make_async_remote_copy(
        src_ref=src,
        dst_ref=dst,
        send_sem=send_sem,
        recv_sem=recv_sem,
        device_id=device,
        device_id_type=MESH,
    )


def kernel(
    wave,
    length_ref,
    coarse_hbm,
    fine_hbm,
    weight_hbm,
    bias,
    head,
    out_wave,
    out_first,
    out_head,
    gathered,
    coarse,
    fine,
    weight,
    table,
    padded,
    rows,
    spectrum,
    preact,
    disc_delta,
    gen_delta,
    spec_delta,
    grad,
    grad_low,
    core_in,
    kept,
    pair_out,
    pair_in,
    z_out,
    z_in,
    heads,
    heads_mid,
    heads_all,
    core_heads,
    pair_heads,
    zh_out,
    zh_in,
    wave_sum,
    wave_low,
    x_in,
    y_out,
    y_in,
    local_sem,
    gather_send,
    gather_recv,
    core_send,
    core_recv,
    pair_send,
    pair_recv,
    z_send,
    z_recv,
    zh_send,
    zh_recv,
    wave_send,
    wave_recv,
):
    clip = lax.axis_index("clip")
    disc = lax.axis_index("disc")
    core = lax.rem(clip, 2)
    y_lo = lax.rem(clip // 2, 2)
    z = clip // 4
    inner = lax.rem(clip, 4)
    x = lax.rem(disc, X_SIZE)
    y_hi = disc // X_SIZE
    frame, hidden_size = weight.shape
    half = frame // 2
    hop = frame // 4
    frames = padded.shape[1] - 16
    shard = wave.shape[1]
    lanes = 128
    steps = Z_SIZE // 2

    core_peer = {"clip": clip + 1 - 2 * core}
    pair_peer = {"clip": clip + 2 - 4 * y_lo}
    z_up = {"clip": lax.rem(z + 1, Z_SIZE) * 4 + inner}
    z_down = {"clip": lax.rem(z + Z_SIZE - 1, Z_SIZE) * 4 + inner}
    other = lax.rem(disc + X_SIZE, 2 * X_SIZE)
    y_peer = {"disc": other}
    x_at = [lax.rem(x + k, X_SIZE) for k in range(X_SIZE)]
    x_peer = [{"disc": y_hi * X_SIZE + at} for at in x_at]

    coarse_copy = pltpu.make_async_copy(coarse_hbm, coarse, local_sem.at[0])
    fine_copy = pltpu.make_async_copy(fine_hbm, fine, local_sem.at[1])
    weight_copy = pltpu.make_async_copy(weight_hbm, weight, local_sem.at[2])
    barrier = pltpu.get_barrier_semaphore()
    peers = [y_peer, x_peer[2], x_peer[1], x_peer[3], z_up, z_down, pair_peer, core_peer]
    for peer in peers:
        pl.semaphore_signal(barrier, inc=1, device_id=peer, device_id_type=MESH)
    coarse_copy.start()
    fine_copy.start()
    weight_copy.start()
    gathered[disc] = wave[...]
    padded[:, 0:8, :] = jnp.zeros((2, 8, hop), F32)
    padded[:, frames + 8 : frames + 16, :] = jnp.zeros((2, 8, hop), F32)
    pl.semaphore_wait(barrier, len(peers))

    def gather_copy(slot, src, at, peer):
        return remote(src, gathered.at[at], gather_send.at[slot], gather_recv.at[slot], peer)

    to_y = gather_copy(0, wave, disc, y_peer)
    to_x = [gather_copy(k, wave, disc, x_peer[k]) for k in (2, 1, 3)]
    for copy in [to_y] + to_x:
        copy.start()

    coarse_copy.wait()
    fine_copy.wait()
    length = length_ref[0]
    start = lax.shift_right_arithmetic(frame - length, 1)
    length_float = length.astype(F32)
    groups = frame // GROUP

    def table_rows(g):
        row = pl.multiple_of(g * GROUP, GROUP)
        position = lax.broadcasted_iota(jnp.int32, (GROUP, lanes), 0) + (row - start)
        inside = (position >= 0) & (position < length)
        phase = 2.0 * jnp.pi * position.astype(F32) / length_float
        window = jnp.where(inside, 0.5 - 0.5 * jnp.cos(phase), 0.0)
        factor = window * (1.0 / math.sqrt(frame))
        for q in range(half // lanes):
            at = slice(q * lanes, (q + 1) * lanes)
            cos_a = coarse[g, :, at]
            sin_a = coarse[groups + g, :, at]
            cos_b = fine[0:GROUP, at]
            sin_b = fine[GROUP : 2 * GROUP, at]
            real = (cos_a * cos_b - sin_a * sin_b) * factor
            imag = -(sin_a * cos_b + cos_a * sin_b) * factor
            table[pl.ds(row, GROUP), at] = real.astype(BF16)
            table[pl.ds(row, GROUP), half + q * lanes : half + (q + 1) * lanes] = imag.astype(BF16)

    pl.loop(0, groups // 2)(table_rows)
    to_y.wait_recv()
    forward = [gather_copy(3 + k, gathered.at[other], other, x_peer[k]) for k in (2, 1, 3)]
    for copy in forward:
        copy.start()
    pl.loop(groups // 2, groups)(table_rows)
    for copy in to_x + forward:
        copy.wait_recv()

    for j in range(2 * X_SIZE):
        for ch in range(2):
            padded[ch, 8 + shard * j : 8 + shard * (j + 1), :] = gathered[j, ch].astype(F32)
    for piece in range(4):
        for ch in range(2):
            rows[ch * frames : (ch + 1) * frames, piece * hop : (piece + 1) * hop] = padded[
                ch, 6 + piece : 6 + piece + frames, :
            ].astype(BF16)
    for n in range(4):
        at = slice(n * hop, (n + 1) * hop)
        spectrum[:, at] = jnp.dot(rows[...], table[:, at], preferred_element_type=F32).astype(BF16)
    weight_copy.wait()
    preact[...] = jnp.dot(spectrum[...], weight[...], preferred_element_type=F32)
    head_wide = head[...].astype(F32)
    step = 32

    def delta_rows(i, sums):
        at = pl.ds(pl.multiple_of(i * step, step), step)
        pre = preact[at, :] + bias[...]
        slopes = jnp.where(pre > 0, 1.0, LEAK)
        hidden = (pre * slopes).astype(BF16).astype(F32)
        logits = jnp.sum(hidden * head_wide, axis=1, keepdims=True)
        disc_low = (logits * head_wide * slopes).astype(BF16)
        disc_delta[at, :] = disc_low
        gen_delta[at, :] = (GEN_WEIGHT * (logits - 1.0) * head_wide * slopes).astype(BF16)
        return (
            sums[0] + jnp.sum(logits * hidden, axis=0, keepdims=True),
            sums[1] + jnp.sum(disc_low.astype(F32), axis=0, keepdims=True),
        )

    zero = jnp.zeros((1, hidden_size), F32)
    sums = lax.fori_loop(0, 2 * frames // step, delta_rows, (zero, zero))
    for r in range(hidden_size // lanes):
        for t in range(2):
            heads[r, t : t + 1, :] = sums[t][:, r * lanes : (r + 1) * lanes]

    for n in range(4):
        at = slice(n * hop, (n + 1) * hop)
        part = lax.dot_general(
            spectrum[:, at], disc_delta[...], (((0,), (0,)), ((), ())), preferred_element_type=F32
        ).reshape(Z_SIZE // 4, 2, 2, GROUP, hidden_size)
        grad[n * 4 : (n + 1) * 4] = part
        grad_low[n * 4 : (n + 1) * 4] = part.astype(BF16)

    def target(i):
        s = i // 2
        return lax.rem(z + Z_SIZE // 2 + s + lax.rem(i, 2) * (Z_SIZE - 1 - 2 * s), Z_SIZE)

    def core_copy(i):
        return remote(
            grad_low.at[target(i), :, 1 - core],
            core_in.at[i],
            core_send.at[i],
            core_recv.at[i],
            core_peer,
        )

    def pair_copy(i):
        return remote(pair_out.at[i], pair_in.at[i], pair_send.at[i], pair_recv.at[i], pair_peer)

    core_heads_copy = remote(
        heads, core_heads, core_send.at[Z_SIZE], core_recv.at[Z_SIZE], core_peer
    )
    pair_heads_copy = remote(
        heads_mid, pair_heads, pair_send.at[Z_SIZE], pair_recv.at[Z_SIZE], pair_peer
    )
    core_heads_copy.start()
    pl.loop(0, Z_SIZE)(lambda i: core_copy(i).start())

    spec_delta[...] = lax.dot_general(
        gen_delta[...], weight[...], (((1,), (1,)), ((), ())), preferred_element_type=F32
    ).astype(BF16)
    for piece in (2, 0, 1, 3):
        back = lax.dot_general(
            spec_delta[...],
            table[piece * hop : (piece + 1) * hop, :],
            (((1,), (1,)), ((), ())),
            preferred_element_type=F32,
        ).reshape(2, frames, hop)
        at = slice(6 + piece, 6 + piece + frames)
        if piece == 2:
            wave_sum[:, at, :] = back
        else:
            wave_sum[:, at, :] = wave_sum[:, at, :] + back

    core_heads_copy.wait_recv()
    heads_mid[...] = heads[...] + core_heads[...]
    pair_heads_copy.start()

    @pl.loop(0, Z_SIZE)
    def _(i):
        core_copy(i).wait_recv()
        at = target(i)
        pair_out[i] = (grad[at, 1 - y_lo, core] + core_in[i, 1 - y_lo].astype(F32)).astype(BF16)
        pair_copy(i).start()
        kept[i] = grad[at, y_lo, core] + core_in[i, y_lo].astype(F32)

    for j in range(2 * X_SIZE):
        for ch in range(2):
            wave_low[j // X_SIZE, j % X_SIZE, ch] = wave_sum[
                ch, 8 + shard * j : 8 + shard * (j + 1), :
            ].astype(BF16)

    def x_copy(k):
        return remote(
            wave_low.at[:, x_at[k]],
            x_in.at[k - 1],
            wave_send.at[k - 1],
            wave_recv.at[k - 1],
            x_peer[k],
        )

    y_copy = remote(y_out, y_in, wave_send.at[3], wave_recv.at[3], y_peer)
    for k in (2, 1, 3):
        x_copy(k).start()

    pair_heads_copy.wait_recv()
    heads_all[...] = heads_mid[...] + pair_heads[...]

    def z_copy(i, peer):
        return remote(z_out.at[i], z_in.at[i], z_send.at[i], z_recv.at[i], peer)

    def zh_copy(i, peer):
        return remote(zh_out.at[i], zh_in.at[i], zh_send.at[i], zh_recv.at[i], peer)

    for s in range(steps):
        for up, peer in ((0, z_down), (1, z_up)):
            i = 2 * s + up
            pair_copy(i).wait_recv()
            total = kept[i] + pair_in[i].astype(F32)
            total_heads = heads_all[target(i) // 4]
            if s > 0:
                z_copy(i - 2, peer).wait_recv()
                zh_copy(i - 2, peer).wait_recv()
                total = total + z_in[i - 2].astype(F32)
                total_heads = total_heads + zh_in[i - 2]
            if i == Z_SIZE - 1:
                last, last_heads = total, total_heads
            else:
                z_out[i] = total.astype(BF16)
                z_copy(i, peer).start()
                zh_out[i] = total_heads
                zh_copy(i, peer).start()
        if s == 1:
            for k in (2, 1, 3):
                x_copy(k).wait_recv()

            def x_sum(at):
                total = wave_low[at, x].astype(F32)
                for k in range(3):
                    total = total + x_in[k, at].astype(F32)
                return total

            y_out[...] = x_sum(1 - y_hi).astype(BF16)
            y_copy.start()
            out_wave[...] = x_sum(y_hi)
        if s == 4:
            y_copy.wait_recv()
            out_wave[...] = out_wave[...] + y_in[...].astype(F32)

    i = Z_SIZE - 2
    z_copy(i, z_down).wait_recv()
    zh_copy(i, z_down).wait_recv()
    out_first[...] = last + z_in[i].astype(F32)
    width = 2 * hidden_size // (4 * Z_SIZE * 2)
    shift = lax.rem(lanes - width * lax.rem(clip, lanes // width), lanes)
    total_heads = last_heads + zh_in[i]
    out_head[...] = pltpu.roll(jnp.concatenate([total_heads] * 4, axis=0), shift, axis=1)

    for copy in [to_y] + to_x + forward:
        copy.wait_send()
    core_heads_copy.wait_send()
    pair_heads_copy.wait_send()

    @pl.loop(0, Z_SIZE)
    def _(i):
        core_copy(i).wait_send()
        pair_copy(i).wait_send()

    for i in range(Z_SIZE - 1):
        z_copy(i, z_up).wait_send()
        zh_copy(i, z_up).wait_send()
    for k in (2, 1, 3):
        x_copy(k).wait_send()
    y_copy.wait_send()


def body(waveform, window_length, first_weight, first_bias, head_weight):
    frame, hidden_size = first_weight.shape[1:]
    hop = frame // 4
    shard = waveform.shape[2] // hop
    frames = shard * 2 * X_SIZE
    count = 2 * frames
    block = (GROUP, hidden_size)
    vmem = pl.BlockSpec(memory_space=pltpu.VMEM)
    any_space = pl.BlockSpec(memory_space=pl.ANY)
    coarse, fine = [jnp.asarray(part) for part in twiddles(frame)]
    out_wave, out_first, out_head = pl.pallas_call(
        kernel,
        out_shape=(
            jax.ShapeDtypeStruct((2, shard, hop), F32),
            jax.ShapeDtypeStruct(block, F32),
            jax.ShapeDtypeStruct((8, 128), F32),
        ),
        in_specs=[
            vmem,
            pl.BlockSpec(memory_space=pltpu.SMEM),
            any_space,
            any_space,
            any_space,
            vmem,
            vmem,
        ],
        out_specs=(vmem, vmem, vmem),
        scratch_shapes=[
            pltpu.VMEM((2 * X_SIZE, 2, shard, hop), BF16),
            pltpu.VMEM(coarse.shape, F32),
            pltpu.VMEM(fine.shape, F32),
            pltpu.VMEM((frame, hidden_size), BF16),
            pltpu.VMEM((frame, frame), BF16),
            pltpu.VMEM((2, frames + 16, hop), F32),
            pltpu.VMEM((count, frame), BF16),
            pltpu.VMEM((count, frame), BF16),
            pltpu.VMEM((count, hidden_size), F32),
            pltpu.VMEM((count, hidden_size), BF16),
            pltpu.VMEM((count, hidden_size), BF16),
            pltpu.VMEM((count, frame), BF16),
            pltpu.VMEM((Z_SIZE, 2, 2) + block, F32),
            pltpu.VMEM((Z_SIZE, 2, 2) + block, BF16),
            pltpu.VMEM((Z_SIZE, 2) + block, BF16),
            pltpu.VMEM((Z_SIZE,) + block, F32),
            pltpu.VMEM((Z_SIZE,) + block, BF16),
            pltpu.VMEM((Z_SIZE,) + block, BF16),
            pltpu.VMEM((Z_SIZE,) + block, BF16),
            pltpu.VMEM((Z_SIZE,) + block, BF16),
            pltpu.VMEM((hidden_size // 128, 2, 128), F32),
            pltpu.VMEM((hidden_size // 128, 2, 128), F32),
            pltpu.VMEM((hidden_size // 128, 2, 128), F32),
            pltpu.VMEM((hidden_size // 128, 2, 128), F32),
            pltpu.VMEM((hidden_size // 128, 2, 128), F32),
            pltpu.VMEM((Z_SIZE, 2, 128), F32),
            pltpu.VMEM((Z_SIZE, 2, 128), F32),
            pltpu.VMEM((2, frames + 16, hop), F32),
            pltpu.VMEM((2, X_SIZE, 2, shard, hop), BF16),
            pltpu.VMEM((3, 2, 2, shard, hop), BF16),
            pltpu.VMEM((2, shard, hop), BF16),
            pltpu.VMEM((2, shard, hop), BF16),
            pltpu.SemaphoreType.DMA((3,)),
            pltpu.SemaphoreType.DMA((7,)),
            pltpu.SemaphoreType.DMA((7,)),
            pltpu.SemaphoreType.DMA((Z_SIZE + 1,)),
            pltpu.SemaphoreType.DMA((Z_SIZE + 1,)),
            pltpu.SemaphoreType.DMA((Z_SIZE + 1,)),
            pltpu.SemaphoreType.DMA((Z_SIZE + 1,)),
            pltpu.SemaphoreType.DMA((Z_SIZE,)),
            pltpu.SemaphoreType.DMA((Z_SIZE,)),
            pltpu.SemaphoreType.DMA((Z_SIZE,)),
            pltpu.SemaphoreType.DMA((Z_SIZE,)),
            pltpu.SemaphoreType.DMA((4,)),
            pltpu.SemaphoreType.DMA((4,)),
        ],
        compiler_params=pltpu.CompilerParams(
            collective_id=0, has_side_effects=True, vmem_limit_bytes=48 * 1024 * 1024
        ),
    )(
        waveform.reshape(2, shard, hop),
        window_length,
        coarse,
        fine,
        first_weight[0],
        first_bias,
        head_weight,
    )
    width = 8
    return (
        out_wave.reshape(1, 2, shard * hop),
        out_first[None],
        out_head[:2, :width].T[None],
    )


def solution(mesh):
    placed = (
        P("clip", None, "disc"),
        P("disc"),
        P("disc", None, None),
        P("disc", None),
        P("disc", None),
    )
    return jax.shard_map(
        body,
        mesh=mesh,
        in_specs=placed,
        out_specs=(P("clip", None, "disc"), P("disc", "clip", None), P("disc", "clip", None)),
        check_vma=False,
    )
```

```python
import math

import jax
import jax.numpy as jnp
import numpy as np
from jax import lax
from jax.experimental import pallas as pl
from jax.experimental.pallas import tpu as pltpu
from jax.sharding import PartitionSpec as P

GEN_WEIGHT = 10.0
LEAK = 0.2
MESH = pl.DeviceIdType.MESH
GROUP = 16
X_SIZE = 4
Z_SIZE = 16
F32 = jnp.float32
BF16 = jnp.bfloat16


def twiddles(frame):
    column = np.arange(frame // 2)
    coarse = (np.arange(0, frame, GROUP)[:, None] * column[None, :]) % frame
    fine = (np.arange(GROUP)[:, None] * column[None, :]) % frame
    angle = 2.0 * np.pi / frame
    coarse = np.concatenate([np.cos(coarse * angle), np.sin(coarse * angle)], axis=0)
    fine = np.concatenate([np.cos(fine * angle), np.sin(fine * angle)], axis=0)
    return coarse[:, None, :].astype(np.float32), fine.astype(np.float32)


def cosine(angle):
    square = angle * angle
    total = jnp.full_like(square, 1.0 / math.factorial(16))
    for power in range(14, -1, -2):
        total = 1.0 / math.factorial(power) - total * square
    return total


def remote(src, dst, send_sem, recv_sem, device):
    return pltpu.make_async_remote_copy(
        src_ref=src,
        dst_ref=dst,
        send_sem=send_sem,
        recv_sem=recv_sem,
        device_id=device,
        device_id_type=MESH,
    )


def kernel(
    wave_hbm,
    length_hbm,
    coarse_hbm,
    fine_hbm,
    weight_hbm,
    bias_hbm,
    head_hbm,
    out_wave,
    out_first,
    out_head,
    raw,
    staged,
    wave,
    length_ref,
    bias,
    head,
    gathered,
    coarse,
    fine,
    weight,
    table,
    padded,
    rows,
    spectrum,
    preact,
    disc_delta,
    gen_delta,
    spec_delta,
    grad,
    grad_low,
    core_in,
    kept,
    pair_out,
    pair_in,
    z_out,
    z_in,
    z_own,
    heads,
    heads_mid,
    heads_all,
    core_heads,
    pair_heads,
    zh_in,
    wave_sum,
    wave_low,
    x_in,
    y_out,
    y_in,
    local_sem,
    gather_send,
    gather_recv,
    core_send,
    core_recv,
    pair_send,
    pair_recv,
    z_send,
    z_recv,
    zh_send,
    zh_recv,
    wave_send,
    wave_recv,
    from_down,
    from_up,
):
    clip = lax.axis_index("clip")
    disc = lax.axis_index("disc")
    core = lax.rem(clip, 2)
    y_lo = lax.rem(clip // 2, 2)
    z = clip // 4
    inner = lax.rem(clip, 4)
    x = lax.rem(disc, X_SIZE)
    y_hi = disc // X_SIZE
    frame, hidden_size = weight.shape
    half = frame // 2
    hop = frame // 4
    frames = padded.shape[1] - 16
    shard = wave.shape[1]
    lanes = 128

    core_peer = {"clip": clip + 1 - 2 * core}
    pair_peer = {"clip": clip + 2 - 4 * y_lo}
    z_up = {"clip": lax.rem(z + 1, Z_SIZE) * 4 + inner}
    z_down = {"clip": lax.rem(z + Z_SIZE - 1, Z_SIZE) * 4 + inner}
    other = lax.rem(disc + X_SIZE, 2 * X_SIZE)
    y_peer = {"disc": other}
    x_at = [lax.rem(x + k, X_SIZE) for k in range(X_SIZE)]
    x_peer = [{"disc": y_hi * X_SIZE + at} for at in x_at]

    local = ((wave_hbm, raw), (length_hbm, length_ref), (coarse_hbm, coarse), (fine_hbm, fine))
    local += ((bias_hbm, bias), (head_hbm, head), (weight_hbm, weight))
    copies = [
        pltpu.make_async_copy(src, dst, local_sem.at[i]) for i, (src, dst) in enumerate(local)
    ]
    barrier = pltpu.get_barrier_semaphore()
    peers = [y_peer, x_peer[2], x_peer[1], x_peer[3], z_up, z_down, pair_peer, core_peer]
    for peer in peers:
        pl.semaphore_signal(barrier, inc=1, device_id=peer, device_id_type=MESH)
    for copy in copies:
        copy.start()
    copies[0].wait()
    for h in range(shard):
        part = raw[:, h * hop : (h + 1) * hop].astype(F32)
        for ch in range(2):
            staged[ch, h : h + 1, :] = part[ch : ch + 1, :]
    wave[...] = staged[...].astype(BF16)
    gathered[disc] = staged[...].astype(BF16)
    padded[:, 0:8, :] = jnp.zeros((2, 8, hop), F32)
    padded[:, frames + 8 : frames + 16, :] = jnp.zeros((2, 8, hop), F32)
    pl.semaphore_wait(barrier, len(peers))

    def gather_copy(slot, src, at, peer):
        return remote(src, gathered.at[at], gather_send.at[slot], gather_recv.at[slot], peer)

    to_y = gather_copy(0, wave, disc, y_peer)
    to_x = [gather_copy(k, wave, disc, x_peer[k]) for k in (2, 1, 3)]
    for copy in [to_y] + to_x:
        copy.start()

    for copy in copies[1:4]:
        copy.wait()
    length = length_ref[0]
    start = lax.shift_right_arithmetic(frame - length, 1)
    length_float = length.astype(F32)
    groups = frame // GROUP

    def table_rows(g):
        row = pl.multiple_of(g * GROUP, GROUP)
        position = lax.broadcasted_iota(jnp.int32, (GROUP, lanes), 0) + (row - start)
        inside = (position >= 0) & (position < length)
        angle = jnp.pi * position.astype(F32) / length_float - 0.5 * jnp.pi
        root = cosine(angle)
        factor = jnp.where(inside, root * root * (1.0 / math.sqrt(frame)), 0.0)
        for q in range(half // lanes):
            at = slice(q * lanes, (q + 1) * lanes)
            cos_a = coarse[g, :, at]
            sin_a = coarse[groups + g, :, at]
            cos_b = fine[0:GROUP, at]
            sin_b = fine[GROUP : 2 * GROUP, at]
            real = (cos_a * cos_b - sin_a * sin_b) * factor
            imag = -(sin_a * cos_b + cos_a * sin_b) * factor
            table[pl.ds(row, GROUP), at] = real.astype(BF16)
            table[pl.ds(row, GROUP), half + q * lanes : half + (q + 1) * lanes] = imag.astype(BF16)

    def relay():
        pl.semaphore_signal(from_down, inc=1, device_id=z_up, device_id_type=MESH)
        pl.semaphore_signal(from_up, inc=1, device_id=z_down, device_id_type=MESH)

    def relay_wait():
        pl.semaphore_wait(from_down, 1)
        pl.semaphore_wait(from_up, 1)

    relay()
    pl.loop(0, groups // 2)(table_rows)
    to_y.wait_recv()
    forward = [gather_copy(3 + k, gathered.at[other], other, x_peer[k]) for k in (2, 1, 3)]
    for copy in forward:
        copy.start()
    relay_wait()
    relay()
    pl.loop(groups // 2, groups)(table_rows)
    for copy in to_x + forward:
        copy.wait_recv()
    relay_wait()
    relay()

    for j in range(2 * X_SIZE):
        for ch in range(2):
            padded[ch, 8 + shard * j : 8 + shard * (j + 1), :] = gathered[j, ch].astype(F32)
    for piece in range(4):
        for ch in range(2):
            rows[ch * frames : (ch + 1) * frames, piece * hop : (piece + 1) * hop] = padded[
                ch, 6 + piece : 6 + piece + frames, :
            ].astype(BF16)
    for n in range(4):
        at = slice(n * hop, (n + 1) * hop)
        spectrum[:, at] = jnp.dot(rows[...], table[:, at], preferred_element_type=F32).astype(BF16)
    for copy in copies[4:]:
        copy.wait()
    relay_wait()
    relay()
    preact[...] = jnp.dot(spectrum[...], weight[...], preferred_element_type=F32)
    head_wide = head[...].astype(F32)
    step = 32

    def delta_rows(i, sums):
        at = pl.ds(pl.multiple_of(i * step, step), step)
        pre = preact[at, :] + bias[...]
        slopes = jnp.where(pre > 0, 1.0, LEAK)
        hidden = (pre * slopes).astype(BF16).astype(F32)
        logits = jnp.sum(hidden * head_wide, axis=1, keepdims=True)
        disc_low = (logits * head_wide * slopes).astype(BF16)
        disc_delta[at, :] = disc_low
        gen_delta[at, :] = (GEN_WEIGHT * (logits - 1.0) * head_wide * slopes).astype(BF16)
        return (
            sums[0] + jnp.sum(logits * hidden, axis=0, keepdims=True),
            sums[1] + jnp.sum(disc_low.astype(F32), axis=0, keepdims=True),
        )

    zero = jnp.zeros((1, hidden_size), F32)
    sums = lax.fori_loop(0, 2 * frames // step, delta_rows, (zero, zero))
    for r in range(hidden_size // lanes):
        for t in range(2):
            heads[r, t : t + 1, :] = sums[t][:, r * lanes : (r + 1) * lanes]

    for n in range(4):
        at = slice(n * hop, (n + 1) * hop)
        part = lax.dot_general(
            spectrum[:, at], disc_delta[...], (((0,), (0,)), ((), ())), preferred_element_type=F32
        ).reshape(Z_SIZE // 4, 2, 2, GROUP, hidden_size)
        grad[n * 4 : (n + 1) * 4] = part
        grad_low[n * 4 : (n + 1) * 4] = part.astype(BF16)

    relay_wait()
    relay()

    def core_copy(i):
        return remote(
            grad_low.at[i, :, 1 - core],
            core_in.at[i],
            core_send.at[i],
            core_recv.at[i],
            core_peer,
        )

    def pair_copy(i):
        return remote(pair_out.at[i], pair_in.at[i], pair_send.at[i], pair_recv.at[i], pair_peer)

    core_heads_copy = remote(
        heads, core_heads, core_send.at[Z_SIZE], core_recv.at[Z_SIZE], core_peer
    )
    pair_heads_copy = remote(
        heads_mid, pair_heads, pair_send.at[Z_SIZE], pair_recv.at[Z_SIZE], pair_peer
    )
    core_heads_copy.start()
    pl.loop(0, Z_SIZE)(lambda i: core_copy(i).start())

    spec_delta[...] = lax.dot_general(
        gen_delta[...], weight[...], (((1,), (1,)), ((), ())), preferred_element_type=F32
    ).astype(BF16)
    for piece in (2, 0, 1, 3):
        back = lax.dot_general(
            spec_delta[...],
            table[piece * hop : (piece + 1) * hop, :],
            (((1,), (1,)), ((), ())),
            preferred_element_type=F32,
        ).reshape(2, frames, hop)
        at = slice(6 + piece, 6 + piece + frames)
        if piece == 2:
            wave_sum[:, at, :] = back
        else:
            wave_sum[:, at, :] = wave_sum[:, at, :] + back

    relay_wait()
    relay()

    core_heads_copy.wait_recv()
    heads_mid[...] = heads[...] + core_heads[...]
    pair_heads_copy.start()

    @pl.loop(0, Z_SIZE)
    def _(i):
        core_copy(i).wait_recv()
        pair_out[i] = (grad[i, 1 - y_lo, core] + core_in[i, 1 - y_lo].astype(F32)).astype(BF16)
        pair_copy(i).start()
        kept[i] = grad[i, y_lo, core] + core_in[i, y_lo].astype(F32)

    relay_wait()
    relay()

    for j in range(2 * X_SIZE):
        for ch in range(2):
            wave_low[j // X_SIZE, j % X_SIZE, ch] = wave_sum[
                ch, 8 + shard * j : 8 + shard * (j + 1), :
            ].astype(BF16)

    def x_copy(k):
        return remote(
            wave_low.at[:, x_at[k]],
            x_in.at[k - 1],
            wave_send.at[k - 1],
            wave_recv.at[k - 1],
            x_peer[k],
        )

    y_copy = remote(y_out, y_in, wave_send.at[3], wave_recv.at[3], y_peer)
    for k in (2, 1, 3):
        x_copy(k).start()

    pair_heads_copy.wait_recv()
    heads_all[...] = heads_mid[...] + pair_heads[...]
    relay_wait()

    def z_copy(to, slot):
        peer = {"clip": to * 4 + inner}
        return remote(z_out.at[to], z_in.at[slot], z_send.at[to], z_recv.at[slot], peer)

    def zh_copy(to, slot):
        peer = {"clip": to * 4 + inner}
        return remote(heads_all.at[to // 4], zh_in.at[slot], zh_send.at[to], zh_recv.at[slot], peer)

    @pl.loop(0, Z_SIZE)
    def _(i):
        pair_copy(i).wait_recv()
        total = kept[i] + pair_in[i].astype(F32)

        @pl.when(i != z)
        def _():
            z_out[i] = total.astype(BF16)
            z_copy(i, z).start()
            zh_copy(i, z).start()

        @pl.when(i == z)
        def _():
            z_own[...] = total

    for k in (2, 1, 3):
        x_copy(k).wait_recv()

    def x_sum(at):
        total = wave_low[at, x].astype(F32)
        for k in range(3):
            total = total + x_in[k, at].astype(F32)
        return total

    y_out[...] = x_sum(1 - y_hi).astype(BF16)
    y_copy.start()
    out_wave[...] = x_sum(y_hi)
    z_in[z] = jnp.zeros((GROUP, hidden_size), BF16)
    zh_in[z] = heads_all[z // 4]
    y_copy.wait_recv()
    out_wave[...] = out_wave[...] + y_in[...].astype(F32)

    @pl.loop(0, Z_SIZE)
    def _(i):
        @pl.when(i != z)
        def _():
            z_copy(i, i).wait_recv()
            zh_copy(i, i).wait_recv()

    total = z_own[...]
    total_heads = zh_in[0]
    for i in range(Z_SIZE):
        total = total + z_in[i].astype(F32)
        if i > 0:
            total_heads = total_heads + zh_in[i]
    out_first[...] = total
    width = hidden_size // (4 * Z_SIZE)
    shift = lax.rem(lanes - width * lax.rem(clip, lanes // width), lanes)
    out_head[...] = pltpu.roll(jnp.concatenate([total_heads] * 4, axis=0), shift, axis=1)

    for copy in [to_y] + to_x + forward:
        copy.wait_send()
    core_heads_copy.wait_send()
    pair_heads_copy.wait_send()

    @pl.loop(0, Z_SIZE)
    def _(i):
        core_copy(i).wait_send()
        pair_copy(i).wait_send()

    @pl.loop(0, Z_SIZE)
    def _(i):
        @pl.when(i != z)
        def _():
            z_copy(i, z).wait_send()
            zh_copy(i, z).wait_send()

    for k in (2, 1, 3):
        x_copy(k).wait_send()
    y_copy.wait_send()


def body(waveform, window_length, first_weight, first_bias, head_weight):
    frame, hidden_size = first_weight.shape[1:]
    hop = frame // 4
    shard = waveform.shape[2] // hop
    frames = shard * 2 * X_SIZE
    count = 2 * frames
    block = (GROUP, hidden_size)
    vmem = pl.BlockSpec(memory_space=pltpu.VMEM)
    hbm = pl.BlockSpec(memory_space=pltpu.HBM)
    coarse, fine = [jnp.asarray(part) for part in twiddles(frame)]
    out_wave, out_first, out_head = pl.pallas_call(
        kernel,
        out_shape=(
            jax.ShapeDtypeStruct((2, shard, hop), F32),
            jax.ShapeDtypeStruct(block, F32),
            jax.ShapeDtypeStruct((8, 128), F32),
        ),
        in_specs=[hbm] * 7,
        out_specs=(vmem, vmem, vmem),
        scratch_shapes=[
            pltpu.VMEM((2, shard * hop), BF16),
            pltpu.VMEM((2, shard, hop), F32),
            pltpu.VMEM((2, shard, hop), BF16),
            pltpu.SMEM((1,), jnp.int32),
            pltpu.VMEM((1, hidden_size), F32),
            pltpu.VMEM((1, hidden_size), BF16),
            pltpu.VMEM((2 * X_SIZE, 2, shard, hop), BF16),
            pltpu.VMEM(coarse.shape, F32),
            pltpu.VMEM(fine.shape, F32),
            pltpu.VMEM((frame, hidden_size), BF16),
            pltpu.VMEM((frame, frame), BF16),
            pltpu.VMEM((2, frames + 16, hop), F32),
            pltpu.VMEM((count, frame), BF16),
            pltpu.VMEM((count, frame), BF16),
            pltpu.VMEM((count, hidden_size), F32),
            pltpu.VMEM((count, hidden_size), BF16),
            pltpu.VMEM((count, hidden_size), BF16),
            pltpu.VMEM((count, frame), BF16),
            pltpu.VMEM((Z_SIZE, 2, 2) + block, F32),
            pltpu.VMEM((Z_SIZE, 2, 2) + block, BF16),
            pltpu.VMEM((Z_SIZE, 2) + block, BF16),
            pltpu.VMEM((Z_SIZE,) + block, F32),
            pltpu.VMEM((Z_SIZE,) + block, BF16),
            pltpu.VMEM((Z_SIZE,) + block, BF16),
            pltpu.VMEM((Z_SIZE,) + block, BF16),
            pltpu.VMEM((Z_SIZE,) + block, BF16),
            pltpu.VMEM(block, F32),
            pltpu.VMEM((hidden_size // 128, 2, 128), F32),
            pltpu.VMEM((hidden_size // 128, 2, 128), F32),
            pltpu.VMEM((hidden_size // 128, 2, 128), F32),
            pltpu.VMEM((hidden_size // 128, 2, 128), F32),
            pltpu.VMEM((hidden_size // 128, 2, 128), F32),
            pltpu.VMEM((Z_SIZE, 2, 128), F32),
            pltpu.VMEM((2, frames + 16, hop), F32),
            pltpu.VMEM((2, X_SIZE, 2, shard, hop), BF16),
            pltpu.VMEM((3, 2, 2, shard, hop), BF16),
            pltpu.VMEM((2, shard, hop), BF16),
            pltpu.VMEM((2, shard, hop), BF16),
            pltpu.SemaphoreType.DMA((7,)),
            pltpu.SemaphoreType.DMA((7,)),
            pltpu.SemaphoreType.DMA((7,)),
            pltpu.SemaphoreType.DMA((Z_SIZE + 1,)),
            pltpu.SemaphoreType.DMA((Z_SIZE + 1,)),
            pltpu.SemaphoreType.DMA((Z_SIZE + 1,)),
            pltpu.SemaphoreType.DMA((Z_SIZE + 1,)),
            pltpu.SemaphoreType.DMA((Z_SIZE,)),
            pltpu.SemaphoreType.DMA((Z_SIZE,)),
            pltpu.SemaphoreType.DMA((Z_SIZE,)),
            pltpu.SemaphoreType.DMA((Z_SIZE,)),
            pltpu.SemaphoreType.DMA((4,)),
            pltpu.SemaphoreType.DMA((4,)),
            pltpu.SemaphoreType.REGULAR,
            pltpu.SemaphoreType.REGULAR,
        ],
        compiler_params=pltpu.CompilerParams(
            collective_id=0, has_side_effects=True, vmem_limit_bytes=48 * 1024 * 1024
        ),
    )(
        waveform[0],
        window_length,
        coarse,
        fine,
        first_weight[0],
        first_bias,
        head_weight,
    )
    width = 8
    return (
        out_wave.reshape(1, 2, shard * hop),
        out_first[None],
        out_head[:2, :width].T[None],
    )


def solution(mesh):
    placed = (
        P("clip", None, "disc"),
        P("disc"),
        P("disc", None, None),
        P("disc", None),
        P("disc", None),
    )
    return jax.shard_map(
        body,
        mesh=mesh,
        in_specs=placed,
        out_specs=(P("clip", None, "disc"), P("disc", "clip", None), P("disc", "clip", None)),
        check_vma=False,
    )
```

```python
import math

import jax
import jax.numpy as jnp
import numpy as np
from jax import lax
from jax.experimental import pallas as pl
from jax.experimental.pallas import tpu as pltpu
from jax.sharding import PartitionSpec as P

GEN_WEIGHT = 10.0
LEAK = 0.2
MESH = pl.DeviceIdType.MESH
GROUP = 16
X_SIZE = 4
Z_SIZE = 16
F32 = jnp.float32
BF16 = jnp.bfloat16


def twiddles(frame):
    column = np.arange(frame // 2)
    coarse = (np.arange(0, frame, GROUP)[:, None] * column[None, :]) % frame
    fine = (np.arange(GROUP)[:, None] * column[None, :]) % frame
    angle = 2.0 * np.pi / frame
    coarse = np.concatenate([np.cos(coarse * angle), np.sin(coarse * angle)], axis=0)
    fine = np.concatenate([np.cos(fine * angle), np.sin(fine * angle)], axis=0)
    return coarse[:, None, :].astype(np.float32), fine.astype(np.float32)


def cosine(angle):
    square = angle * angle
    total = jnp.full_like(square, 1.0 / math.factorial(16))
    for power in range(14, -1, -2):
        total = 1.0 / math.factorial(power) - total * square
    return total


def remote(src, dst, send_sem, recv_sem, device):
    return pltpu.make_async_remote_copy(
        src_ref=src,
        dst_ref=dst,
        send_sem=send_sem,
        recv_sem=recv_sem,
        device_id=device,
        device_id_type=MESH,
    )


def kernel(
    length_ref,
    wave_hbm,
    coarse_hbm,
    fine_hbm,
    weight_hbm,
    bias_hbm,
    head_hbm,
    out_wave,
    out_first,
    out_head,
    raw,
    staged,
    wave,
    bias,
    head,
    gathered,
    coarse,
    fine,
    weight,
    table,
    padded,
    rows,
    spectrum,
    preact,
    disc_delta,
    gen_delta,
    spec_delta,
    grad,
    grad_low,
    core_in,
    kept,
    pair_out,
    pair_in,
    z_out,
    z_in,
    z_own,
    heads,
    heads_mid,
    heads_all,
    core_heads,
    pair_heads,
    zh_in,
    wave_sum,
    wave_low,
    x_in,
    y_out,
    y_in,
    local_sem,
    gather_send,
    gather_recv,
    core_send,
    core_recv,
    pair_send,
    pair_recv,
    z_send,
    z_recv,
    zh_send,
    zh_recv,
    wave_send,
    wave_recv,
    near_sem,
):
    clip = lax.axis_index("clip")
    disc = lax.axis_index("disc")
    core = lax.rem(clip, 2)
    y_lo = lax.rem(clip // 2, 2)
    z = clip // 4
    inner = lax.rem(clip, 4)
    x = lax.rem(disc, X_SIZE)
    y_hi = disc // X_SIZE
    frame, hidden_size = weight.shape
    half = frame // 2
    hop = frame // 4
    frames = padded.shape[1] - 16
    shard = wave.shape[1]
    lanes = 128

    core_peer = {"clip": clip + 1 - 2 * core}
    pair_peer = {"clip": clip + 2 - 4 * y_lo}
    z_near = [
        {"clip": lax.rem(z + away, Z_SIZE) * 4 + inner} for away in (1, 2, Z_SIZE - 1, Z_SIZE - 2)
    ]
    other = lax.rem(disc + X_SIZE, 2 * X_SIZE)
    y_peer = {"disc": other}
    x_at = [lax.rem(x + k, X_SIZE) for k in range(X_SIZE)]
    x_peer = [{"disc": y_hi * X_SIZE + at} for at in x_at]

    local = ((wave_hbm, raw), (coarse_hbm, coarse), (fine_hbm, fine))
    local += ((bias_hbm, bias), (head_hbm, head), (weight_hbm, weight))
    copies = [
        pltpu.make_async_copy(src, dst, local_sem.at[i]) for i, (src, dst) in enumerate(local)
    ]
    barrier = pltpu.get_barrier_semaphore()
    peers = [y_peer, x_peer[2], x_peer[1], x_peer[3], *z_near, pair_peer, core_peer]
    for peer in peers:
        pl.semaphore_signal(barrier, inc=1, device_id=peer, device_id_type=MESH)
    for copy in copies:
        copy.start()
    copies[0].wait()
    for h in range(shard):
        part = raw[:, h * hop : (h + 1) * hop].astype(F32)
        for ch in range(2):
            staged[ch, h : h + 1, :] = part[ch : ch + 1, :]
    wave[...] = staged[...].astype(BF16)
    gathered[disc] = staged[...].astype(BF16)
    padded[:, 0:8, :] = jnp.zeros((2, 8, hop), F32)
    padded[:, frames + 8 : frames + 16, :] = jnp.zeros((2, 8, hop), F32)
    pl.semaphore_wait(barrier, len(peers))

    def gather_copy(slot, src, at, peer):
        return remote(src, gathered.at[at], gather_send.at[slot], gather_recv.at[slot], peer)

    to_y = gather_copy(0, wave, disc, y_peer)
    to_x = [gather_copy(k, wave, disc, x_peer[k]) for k in (2, 1, 3)]
    for copy in [to_y] + to_x:
        copy.start()

    for copy in copies[1:3]:
        copy.wait()
    length = length_ref[0]
    start = lax.shift_right_arithmetic(frame - length, 1)
    length_float = length.astype(F32)
    groups = frame // GROUP

    def table_rows(g):
        row = pl.multiple_of(g * GROUP, GROUP)
        position = lax.broadcasted_iota(jnp.int32, (GROUP, lanes), 0) + (row - start)
        inside = (position >= 0) & (position < length)
        angle = jnp.pi * position.astype(F32) / length_float - 0.5 * jnp.pi
        root = cosine(angle)
        factor = jnp.where(inside, root * root * (1.0 / math.sqrt(frame)), 0.0)
        for q in range(half // lanes):
            at = slice(q * lanes, (q + 1) * lanes)
            cos_a = coarse[g, :, at]
            sin_a = coarse[groups + g, :, at]
            cos_b = fine[0:GROUP, at]
            sin_b = fine[GROUP : 2 * GROUP, at]
            real = (cos_a * cos_b - sin_a * sin_b) * factor
            imag = -(sin_a * cos_b + cos_a * sin_b) * factor
            table[pl.ds(row, GROUP), at] = real.astype(BF16)
            table[pl.ds(row, GROUP), half + q * lanes : half + (q + 1) * lanes] = imag.astype(BF16)

    def relay(turn):
        for peer in z_near:
            pl.semaphore_signal(near_sem.at[turn], inc=1, device_id=peer, device_id_type=MESH)

    def relay_wait(turn):
        pl.semaphore_wait(near_sem.at[turn], len(z_near))

    relay(0)
    pl.loop(0, groups // 2)(table_rows)
    to_y.wait_recv()
    forward = [gather_copy(3 + k, gathered.at[other], other, x_peer[k]) for k in (2, 1, 3)]
    for copy in forward:
        copy.start()
    pl.loop(groups // 2, groups)(table_rows)
    for copy in to_x + forward:
        copy.wait_recv()
    for j in range(2 * X_SIZE):
        for ch in range(2):
            padded[ch, 8 + shard * j : 8 + shard * (j + 1), :] = gathered[j, ch].astype(F32)
    for piece in range(4):
        for ch in range(2):
            rows[ch * frames : (ch + 1) * frames, piece * hop : (piece + 1) * hop] = padded[
                ch, 6 + piece : 6 + piece + frames, :
            ].astype(BF16)
    for n in range(4):
        at = slice(n * hop, (n + 1) * hop)
        spectrum[:, at] = jnp.dot(rows[...], table[:, at], preferred_element_type=F32).astype(BF16)
    for copy in copies[3:]:
        copy.wait()
    preact[...] = jnp.dot(spectrum[...], weight[...], preferred_element_type=F32)
    head_wide = head[...].astype(F32)
    step = 32

    def delta_rows(i, sums):
        at = pl.ds(pl.multiple_of(i * step, step), step)
        pre = preact[at, :] + bias[...]
        slopes = jnp.where(pre > 0, 1.0, LEAK)
        hidden = (pre * slopes).astype(BF16).astype(F32)
        logits = jnp.sum(hidden * head_wide, axis=1, keepdims=True)
        disc_low = (logits * head_wide * slopes).astype(BF16)
        disc_delta[at, :] = disc_low
        gen_delta[at, :] = (GEN_WEIGHT * (logits - 1.0) * head_wide * slopes).astype(BF16)
        return (
            sums[0] + jnp.sum(logits * hidden, axis=0, keepdims=True),
            sums[1] + jnp.sum(disc_low.astype(F32), axis=0, keepdims=True),
        )

    zero = jnp.zeros((1, hidden_size), F32)
    sums = lax.fori_loop(0, 2 * frames // step, delta_rows, (zero, zero))
    for r in range(hidden_size // lanes):
        for t in range(2):
            heads[r, t : t + 1, :] = sums[t][:, r * lanes : (r + 1) * lanes]

    for n in range(4):
        at = slice(n * hop, (n + 1) * hop)
        part = lax.dot_general(
            spectrum[:, at], disc_delta[...], (((0,), (0,)), ((), ())), preferred_element_type=F32
        ).reshape(Z_SIZE // 4, 2, 2, GROUP, hidden_size)
        grad[n * 4 : (n + 1) * 4] = part
        grad_low[n * 4 : (n + 1) * 4] = part.astype(BF16)

    def core_copy(i):
        return remote(
            grad_low.at[i, :, 1 - core],
            core_in.at[i],
            core_send.at[i],
            core_recv.at[i],
            core_peer,
        )

    def pair_copy(i):
        return remote(pair_out.at[i], pair_in.at[i], pair_send.at[i], pair_recv.at[i], pair_peer)

    core_heads_copy = remote(
        heads, core_heads, core_send.at[Z_SIZE], core_recv.at[Z_SIZE], core_peer
    )
    pair_heads_copy = remote(
        heads_mid, pair_heads, pair_send.at[Z_SIZE], pair_recv.at[Z_SIZE], pair_peer
    )
    core_heads_copy.start()
    pl.loop(0, Z_SIZE)(lambda i: core_copy(i).start())

    relay_wait(0)
    relay(1)

    spec_delta[...] = lax.dot_general(
        gen_delta[...], weight[...], (((1,), (1,)), ((), ())), preferred_element_type=F32
    ).astype(BF16)
    for piece in (2, 0, 1, 3):
        back = lax.dot_general(
            spec_delta[...],
            table[piece * hop : (piece + 1) * hop, :],
            (((1,), (1,)), ((), ())),
            preferred_element_type=F32,
        ).reshape(2, frames, hop)
        at = slice(6 + piece, 6 + piece + frames)
        if piece == 2:
            wave_sum[:, at, :] = back
        else:
            wave_sum[:, at, :] = wave_sum[:, at, :] + back

    relay_wait(1)
    relay(2)

    core_heads_copy.wait_recv()
    heads_mid[...] = heads[...] + core_heads[...]
    pair_heads_copy.start()

    @pl.loop(0, Z_SIZE)
    def _(i):
        core_copy(i).wait_recv()
        pair_out[i] = (grad[i, 1 - y_lo, core] + core_in[i, 1 - y_lo].astype(F32)).astype(BF16)
        pair_copy(i).start()
        kept[i] = grad[i, y_lo, core] + core_in[i, y_lo].astype(F32)

    for j in range(2 * X_SIZE):
        for ch in range(2):
            wave_low[j // X_SIZE, j % X_SIZE, ch] = wave_sum[
                ch, 8 + shard * j : 8 + shard * (j + 1), :
            ].astype(BF16)

    def x_copy(k):
        return remote(
            wave_low.at[:, x_at[k]],
            x_in.at[k - 1],
            wave_send.at[k - 1],
            wave_recv.at[k - 1],
            x_peer[k],
        )

    y_copy = remote(y_out, y_in, wave_send.at[3], wave_recv.at[3], y_peer)
    for k in (2, 1, 3):
        x_copy(k).start()

    pair_heads_copy.wait_recv()
    heads_all[...] = heads_mid[...] + pair_heads[...]
    relay_wait(2)

    def z_copy(to, slot):
        peer = {"clip": to * 4 + inner}
        return remote(z_out.at[to], z_in.at[slot], z_send.at[to], z_recv.at[slot], peer)

    def zh_copy(to, slot):
        peer = {"clip": to * 4 + inner}
        return remote(heads_all.at[to // 4], zh_in.at[slot], zh_send.at[to], zh_recv.at[slot], peer)

    @pl.loop(0, Z_SIZE)
    def _(i):
        pair_copy(i).wait_recv()
        total = kept[i] + pair_in[i].astype(F32)

        @pl.when(i != z)
        def _():
            z_out[i] = total.astype(BF16)
            z_copy(i, z).start()
            zh_copy(i, z).start()

        @pl.when(i == z)
        def _():
            z_own[...] = total

    for k in (2, 1, 3):
        x_copy(k).wait_recv()

    def x_sum(at):
        total = wave_low[at, x].astype(F32)
        for k in range(3):
            total = total + x_in[k, at].astype(F32)
        return total

    y_out[...] = x_sum(1 - y_hi).astype(BF16)
    y_copy.start()
    out_wave[...] = x_sum(y_hi)
    z_in[z] = jnp.zeros((GROUP, hidden_size), BF16)
    zh_in[z] = heads_all[z // 4]
    y_copy.wait_recv()
    out_wave[...] = out_wave[...] + y_in[...].astype(F32)

    @pl.loop(0, Z_SIZE)
    def _(i):
        @pl.when(i != z)
        def _():
            z_copy(i, i).wait_recv()
            zh_copy(i, i).wait_recv()

    total = z_own[...]
    total_heads = zh_in[0]
    for i in range(Z_SIZE):
        total = total + z_in[i].astype(F32)
        if i > 0:
            total_heads = total_heads + zh_in[i]
    out_first[...] = total
    width = hidden_size // (4 * Z_SIZE)
    shift = lax.rem(lanes - width * lax.rem(clip, lanes // width), lanes)
    out_head[...] = pltpu.roll(jnp.concatenate([total_heads] * 4, axis=0), shift, axis=1)

    for copy in [to_y] + to_x + forward:
        copy.wait_send()
    core_heads_copy.wait_send()
    pair_heads_copy.wait_send()

    @pl.loop(0, Z_SIZE)
    def _(i):
        core_copy(i).wait_send()
        pair_copy(i).wait_send()

    @pl.loop(0, Z_SIZE)
    def _(i):
        @pl.when(i != z)
        def _():
            z_copy(i, z).wait_send()
            zh_copy(i, z).wait_send()

    for k in (2, 1, 3):
        x_copy(k).wait_send()
    y_copy.wait_send()


def body(waveform, window_length, first_weight, first_bias, head_weight):
    frame, hidden_size = first_weight.shape[1:]
    hop = frame // 4
    shard = waveform.shape[2] // hop
    frames = shard * 2 * X_SIZE
    count = 2 * frames
    block = (GROUP, hidden_size)
    vmem = pl.BlockSpec(memory_space=pltpu.VMEM)
    hbm = pl.BlockSpec(memory_space=pltpu.HBM)
    coarse, fine = [jnp.asarray(part) for part in twiddles(frame)]
    operands = (waveform[0], coarse, fine, first_weight[0], first_bias, head_weight)
    out_wave, out_first, out_head = pl.pallas_call(
        kernel,
        out_shape=(
            jax.ShapeDtypeStruct((2, shard, hop), F32),
            jax.ShapeDtypeStruct(block, F32),
            jax.ShapeDtypeStruct((8, 128), F32),
        ),
        in_specs=[pl.BlockSpec(memory_space=pltpu.SMEM)] + [hbm] * len(operands),
        out_specs=(vmem, vmem, vmem),
        scratch_shapes=[
            pltpu.VMEM((2, shard * hop), BF16),
            pltpu.VMEM((2, shard, hop), F32),
            pltpu.VMEM((2, shard, hop), BF16),
            pltpu.VMEM((1, hidden_size), F32),
            pltpu.VMEM((1, hidden_size), BF16),
            pltpu.VMEM((2 * X_SIZE, 2, shard, hop), BF16),
            pltpu.VMEM(coarse.shape, F32),
            pltpu.VMEM(fine.shape, F32),
            pltpu.VMEM((frame, hidden_size), BF16),
            pltpu.VMEM((frame, frame), BF16),
            pltpu.VMEM((2, frames + 16, hop), F32),
            pltpu.VMEM((count, frame), BF16),
            pltpu.VMEM((count, frame), BF16),
            pltpu.VMEM((count, hidden_size), F32),
            pltpu.VMEM((count, hidden_size), BF16),
            pltpu.VMEM((count, hidden_size), BF16),
            pltpu.VMEM((count, frame), BF16),
            pltpu.VMEM((Z_SIZE, 2, 2) + block, F32),
            pltpu.VMEM((Z_SIZE, 2, 2) + block, BF16),
            pltpu.VMEM((Z_SIZE, 2) + block, BF16),
            pltpu.VMEM((Z_SIZE,) + block, F32),
            pltpu.VMEM((Z_SIZE,) + block, BF16),
            pltpu.VMEM((Z_SIZE,) + block, BF16),
            pltpu.VMEM((Z_SIZE,) + block, BF16),
            pltpu.VMEM((Z_SIZE,) + block, BF16),
            pltpu.VMEM(block, F32),
            pltpu.VMEM((hidden_size // 128, 2, 128), F32),
            pltpu.VMEM((hidden_size // 128, 2, 128), F32),
            pltpu.VMEM((hidden_size // 128, 2, 128), F32),
            pltpu.VMEM((hidden_size // 128, 2, 128), F32),
            pltpu.VMEM((hidden_size // 128, 2, 128), F32),
            pltpu.VMEM((Z_SIZE, 2, 128), F32),
            pltpu.VMEM((2, frames + 16, hop), F32),
            pltpu.VMEM((2, X_SIZE, 2, shard, hop), BF16),
            pltpu.VMEM((3, 2, 2, shard, hop), BF16),
            pltpu.VMEM((2, shard, hop), BF16),
            pltpu.VMEM((2, shard, hop), BF16),
            pltpu.SemaphoreType.DMA((6,)),
            pltpu.SemaphoreType.DMA((7,)),
            pltpu.SemaphoreType.DMA((7,)),
            pltpu.SemaphoreType.DMA((Z_SIZE + 1,)),
            pltpu.SemaphoreType.DMA((Z_SIZE + 1,)),
            pltpu.SemaphoreType.DMA((Z_SIZE + 1,)),
            pltpu.SemaphoreType.DMA((Z_SIZE + 1,)),
            pltpu.SemaphoreType.DMA((Z_SIZE,)),
            pltpu.SemaphoreType.DMA((Z_SIZE,)),
            pltpu.SemaphoreType.DMA((Z_SIZE,)),
            pltpu.SemaphoreType.DMA((Z_SIZE,)),
            pltpu.SemaphoreType.DMA((4,)),
            pltpu.SemaphoreType.DMA((4,)),
            pltpu.SemaphoreType.REGULAR((3,)),
        ],
        compiler_params=pltpu.CompilerParams(
            collective_id=0, has_side_effects=True, vmem_limit_bytes=53000 * 1024
        ),
    )(window_length, *[pltpu.with_memory_space_constraint(part, pltpu.HBM) for part in operands])
    width = 8
    return (
        out_wave.reshape(1, 2, shard * hop),
        out_first[None],
        out_head[:2, :width].T[None],
    )


def solution(mesh):
    placed = (
        P("clip", None, "disc"),
        P("disc"),
        P("disc", None, None),
        P("disc", None),
        P("disc", None),
    )
    return jax.shard_map(
        body,
        mesh=mesh,
        in_specs=placed,
        out_specs=(P("clip", None, "disc"), P("disc", "clip", None), P("disc", "clip", None)),
        check_vma=False,
    )
```

```python
import math

import jax
import jax.numpy as jnp
import numpy as np
from jax import lax
from jax.experimental import pallas as pl
from jax.experimental.pallas import tpu as pltpu
from jax.sharding import PartitionSpec as P

GEN_WEIGHT = 10.0
LEAK = 0.2
MESH = pl.DeviceIdType.MESH
GROUP = 16
X_SIZE = 4
Z_SIZE = 16
F32 = jnp.float32
BF16 = jnp.bfloat16


def twiddles(frame):
    column = np.arange(frame // 2)
    coarse = (np.arange(0, frame, GROUP)[:, None] * column[None, :]) % frame
    fine = (np.arange(GROUP)[:, None] * column[None, :]) % frame
    angle = 2.0 * np.pi / frame
    coarse = np.concatenate([np.cos(coarse * angle), np.sin(coarse * angle)], axis=0)
    fine = np.concatenate([np.cos(fine * angle), np.sin(fine * angle)], axis=0)
    return coarse[:, None, :].astype(np.float32), fine.astype(np.float32)


def cosine(angle):
    square = angle * angle
    total = jnp.full_like(square, 1.0 / math.factorial(16))
    for power in range(14, -1, -2):
        total = 1.0 / math.factorial(power) - total * square
    return total


def remote(src, dst, send_sem, recv_sem, device):
    return pltpu.make_async_remote_copy(
        src_ref=src,
        dst_ref=dst,
        send_sem=send_sem,
        recv_sem=recv_sem,
        device_id=device,
        device_id_type=MESH,
    )


def kernel(
    length_ref,
    wave_hbm,
    coarse_hbm,
    fine_hbm,
    weight_hbm,
    bias_hbm,
    head_hbm,
    out_wave,
    out_first,
    out_head,
    raw,
    staged,
    wave,
    bias,
    head,
    gathered,
    coarse,
    fine,
    weight,
    table,
    padded,
    rows,
    spectrum,
    preact,
    disc_delta,
    gen_delta,
    spec_delta,
    grad,
    grad_low,
    core_in,
    kept,
    pair_out,
    pair_in,
    z_out,
    z_in,
    z_own,
    heads,
    heads_mid,
    heads_all,
    core_heads,
    pair_heads,
    zh_in,
    wave_sum,
    wave_low,
    x_in,
    y_out,
    y_in,
    local_sem,
    gather_send,
    gather_recv,
    core_send,
    core_recv,
    pair_send,
    pair_recv,
    z_send,
    z_recv,
    zh_send,
    zh_recv,
    wave_send,
    wave_recv,
    near_sem,
):
    clip = lax.axis_index("clip")
    disc = lax.axis_index("disc")
    core = lax.rem(clip, 2)
    y_lo = lax.rem(clip // 2, 2)
    z = clip // 4
    inner = lax.rem(clip, 4)
    x = lax.rem(disc, X_SIZE)
    y_hi = disc // X_SIZE
    frame, hidden_size = weight.shape
    half = frame // 2
    hop = frame // 4
    frames = padded.shape[1] - 16
    shard = wave.shape[1]
    lanes = 128

    core_peer = {"clip": clip + 1 - 2 * core}
    pair_peer = {"clip": clip + 2 - 4 * y_lo}
    z_near = [
        {"clip": lax.rem(z + away, Z_SIZE) * 4 + inner} for away in (1, 2, Z_SIZE - 1, Z_SIZE - 2)
    ]
    other = lax.rem(disc + X_SIZE, 2 * X_SIZE)
    y_peer = {"disc": other}
    x_at = [lax.rem(x + k, X_SIZE) for k in range(X_SIZE)]
    x_peer = [{"disc": y_hi * X_SIZE + at} for at in x_at]

    local = ((wave_hbm, raw), (coarse_hbm, coarse), (fine_hbm, fine))
    local += ((bias_hbm, bias), (head_hbm, head), (weight_hbm, weight))
    copies = [
        pltpu.make_async_copy(src, dst, local_sem.at[i]) for i, (src, dst) in enumerate(local)
    ]
    barrier = pltpu.get_barrier_semaphore()
    peers = [y_peer, x_peer[2], x_peer[1], x_peer[3], *z_near, pair_peer, core_peer]
    copies[0].start()
    for peer in peers:
        pl.semaphore_signal(barrier, inc=1, device_id=peer, device_id_type=MESH)
    for copy in copies[1:]:
        copy.start()
    copies[0].wait()
    for h in range(shard):
        part = raw[:, h * hop : (h + 1) * hop].astype(F32)
        for ch in range(2):
            staged[ch, h : h + 1, :] = part[ch : ch + 1, :]
    wave[...] = staged[...].astype(BF16)
    gathered[disc] = staged[...].astype(BF16)
    padded[:, 0:8, :] = jnp.zeros((2, 8, hop), F32)
    padded[:, frames + 8 : frames + 16, :] = jnp.zeros((2, 8, hop), F32)
    pl.semaphore_wait(barrier, len(peers))

    def gather_copy(slot, src, at, peer):
        return remote(src, gathered.at[at], gather_send.at[slot], gather_recv.at[slot], peer)

    to_y = gather_copy(0, wave, disc, y_peer)
    to_x = [gather_copy(k, wave, disc, x_peer[k]) for k in (2, 1, 3)]
    for copy in [to_y] + to_x:
        copy.start()

    for copy in copies[1:3]:
        copy.wait()
    length = length_ref[0]
    start = lax.shift_right_arithmetic(frame - length, 1)
    length_float = length.astype(F32)
    groups = frame // GROUP

    def table_rows(g):
        row = pl.multiple_of(g * GROUP, GROUP)
        position = lax.broadcasted_iota(jnp.int32, (GROUP, lanes), 0) + (row - start)
        inside = (position >= 0) & (position < length)
        angle = jnp.pi * position.astype(F32) / length_float - 0.5 * jnp.pi
        root = cosine(angle)
        factor = jnp.where(inside, root * root * (1.0 / math.sqrt(frame)), 0.0)
        for q in range(half // lanes):
            at = slice(q * lanes, (q + 1) * lanes)
            cos_a = coarse[g, :, at]
            sin_a = coarse[groups + g, :, at]
            cos_b = fine[0:GROUP, at]
            sin_b = fine[GROUP : 2 * GROUP, at]
            real = (cos_a * cos_b - sin_a * sin_b) * factor
            imag = -(sin_a * cos_b + cos_a * sin_b) * factor
            table[pl.ds(row, GROUP), at] = real.astype(BF16)
            table[pl.ds(row, GROUP), half + q * lanes : half + (q + 1) * lanes] = imag.astype(BF16)

    def relay(turn):
        for peer in z_near:
            pl.semaphore_signal(near_sem.at[turn], inc=1, device_id=peer, device_id_type=MESH)

    def relay_wait(turn):
        pl.semaphore_wait(near_sem.at[turn], len(z_near))

    relay(0)
    pl.loop(0, groups // 2)(table_rows)
    to_y.wait_recv()
    forward = [gather_copy(3 + k, gathered.at[other], other, x_peer[k]) for k in (2, 1, 3)]
    for copy in forward:
        copy.start()
    pl.loop(groups // 2, groups)(table_rows)
    for copy in to_x + forward:
        copy.wait_recv()
    for j in range(2 * X_SIZE):
        for ch in range(2):
            padded[ch, 8 + shard * j : 8 + shard * (j + 1), :] = gathered[j, ch].astype(F32)
    for piece in range(4):
        for ch in range(2):
            rows[ch * frames : (ch + 1) * frames, piece * hop : (piece + 1) * hop] = padded[
                ch, 6 + piece : 6 + piece + frames, :
            ].astype(BF16)
    for n in range(4):
        at = slice(n * hop, (n + 1) * hop)
        spectrum[:, at] = jnp.dot(rows[...], table[:, at], preferred_element_type=F32).astype(BF16)
    for copy in copies[3:]:
        copy.wait()
    preact[...] = jnp.dot(spectrum[...], weight[...], preferred_element_type=F32)
    head_wide = head[...].astype(F32)
    step = 32

    def delta_rows(i, sums):
        at = pl.ds(pl.multiple_of(i * step, step), step)
        pre = preact[at, :] + bias[...]
        slopes = jnp.where(pre > 0, 1.0, LEAK)
        hidden = (pre * slopes).astype(BF16).astype(F32)
        logits = jnp.sum(hidden * head_wide, axis=1, keepdims=True)
        disc_low = (logits * head_wide * slopes).astype(BF16)
        disc_delta[at, :] = disc_low
        gen_delta[at, :] = (GEN_WEIGHT * (logits - 1.0) * head_wide * slopes).astype(BF16)
        return (
            sums[0] + jnp.sum(logits * hidden, axis=0, keepdims=True),
            sums[1] + jnp.sum(disc_low.astype(F32), axis=0, keepdims=True),
        )

    zero = jnp.zeros((1, hidden_size), F32)
    sums = lax.fori_loop(0, 2 * frames // step, delta_rows, (zero, zero))
    for r in range(hidden_size // lanes):
        for t in range(2):
            heads[r, t : t + 1, :] = sums[t][:, r * lanes : (r + 1) * lanes]

    for n in range(4):
        at = slice(n * hop, (n + 1) * hop)
        part = lax.dot_general(
            spectrum[:, at], disc_delta[...], (((0,), (0,)), ((), ())), preferred_element_type=F32
        ).reshape(Z_SIZE // 4, 2, 2, GROUP, hidden_size)
        grad[n * 4 : (n + 1) * 4] = part
        grad_low[n * 4 : (n + 1) * 4] = part.astype(BF16)

    def core_copy(i):
        return remote(
            grad_low.at[i, :, 1 - core],
            core_in.at[i],
            core_send.at[i],
            core_recv.at[i],
            core_peer,
        )

    def pair_copy(i):
        return remote(pair_out.at[i], pair_in.at[i], pair_send.at[i], pair_recv.at[i], pair_peer)

    core_heads_copy = remote(
        heads, core_heads, core_send.at[Z_SIZE], core_recv.at[Z_SIZE], core_peer
    )
    pair_heads_copy = remote(
        heads_mid, pair_heads, pair_send.at[Z_SIZE], pair_recv.at[Z_SIZE], pair_peer
    )
    core_heads_copy.start()
    pl.loop(0, Z_SIZE)(lambda i: core_copy(i).start())

    relay_wait(0)
    relay(1)

    spec_delta[...] = lax.dot_general(
        gen_delta[...], weight[...], (((1,), (1,)), ((), ())), preferred_element_type=F32
    ).astype(BF16)
    for piece in (2, 0, 1, 3):
        back = lax.dot_general(
            spec_delta[...],
            table[piece * hop : (piece + 1) * hop, :],
            (((1,), (1,)), ((), ())),
            preferred_element_type=F32,
        ).reshape(2, frames, hop)
        at = slice(6 + piece, 6 + piece + frames)
        if piece == 2:
            wave_sum[:, at, :] = back
        else:
            wave_sum[:, at, :] = wave_sum[:, at, :] + back

    relay_wait(1)
    relay(2)

    core_heads_copy.wait_recv()
    heads_mid[...] = heads[...] + core_heads[...]
    pair_heads_copy.start()

    @pl.loop(0, Z_SIZE)
    def _(i):
        core_copy(i).wait_recv()
        pair_out[i] = (grad[i, 1 - y_lo, core] + core_in[i, 1 - y_lo].astype(F32)).astype(BF16)
        pair_copy(i).start()
        kept[i] = grad[i, y_lo, core] + core_in[i, y_lo].astype(F32)

    for j in range(2 * X_SIZE):
        for ch in range(2):
            wave_low[j // X_SIZE, j % X_SIZE, ch] = wave_sum[
                ch, 8 + shard * j : 8 + shard * (j + 1), :
            ].astype(BF16)

    def x_copy(k):
        return remote(
            wave_low.at[:, x_at[k]],
            x_in.at[k - 1],
            wave_send.at[k - 1],
            wave_recv.at[k - 1],
            x_peer[k],
        )

    y_copy = remote(y_out, y_in, wave_send.at[3], wave_recv.at[3], y_peer)
    for k in (2, 1, 3):
        x_copy(k).start()

    pair_heads_copy.wait_recv()
    heads_all[...] = heads_mid[...] + pair_heads[...]
    relay_wait(2)

    def z_copy(to, slot):
        peer = {"clip": to * 4 + inner}
        return remote(z_out.at[to], z_in.at[slot], z_send.at[to], z_recv.at[slot], peer)

    def zh_copy(to, slot):
        peer = {"clip": to * 4 + inner}
        return remote(heads_all.at[to // 4], zh_in.at[slot], zh_send.at[to], zh_recv.at[slot], peer)

    @pl.loop(0, Z_SIZE)
    def _(i):
        pair_copy(i).wait_recv()
        total = kept[i] + pair_in[i].astype(F32)

        @pl.when(i != z)
        def _():
            z_out[i] = total.astype(BF16)
            z_copy(i, z).start()
            zh_copy(i, z).start()

        @pl.when(i == z)
        def _():
            z_own[...] = total

    for k in (2, 1, 3):
        x_copy(k).wait_recv()

    def x_sum(at):
        total = wave_low[at, x].astype(F32)
        for k in range(3):
            total = total + x_in[k, at].astype(F32)
        return total

    y_out[...] = x_sum(1 - y_hi).astype(BF16)
    y_copy.start()
    staged[...] = x_sum(y_hi)
    z_in[z] = jnp.zeros((GROUP, hidden_size), BF16)
    zh_in[z] = heads_all[z // 4]
    y_copy.wait_recv()
    staged[...] = staged[...] + y_in[...].astype(F32)
    for h in range(shard):
        for ch in range(2):
            out_wave[ch : ch + 1, h * hop : (h + 1) * hop] = staged[ch, h : h + 1, :]

    for copy in [to_y] + to_x + forward:
        copy.wait_send()
    core_heads_copy.wait_send()
    pair_heads_copy.wait_send()

    @pl.loop(0, Z_SIZE)
    def _(i):
        core_copy(i).wait_send()
        pair_copy(i).wait_send()

    @pl.loop(0, Z_SIZE)
    def _(i):
        @pl.when(i != z)
        def _():
            z_copy(i, z).wait_send()
            zh_copy(i, z).wait_send()

    for k in (2, 1, 3):
        x_copy(k).wait_send()
    y_copy.wait_send()

    @pl.loop(0, Z_SIZE)
    def _(i):
        @pl.when(i != z)
        def _():
            z_copy(i, i).wait_recv()
            zh_copy(i, i).wait_recv()

    total = z_own[...]
    total_heads = zh_in[0]
    for i in range(Z_SIZE):
        total = total + z_in[i].astype(F32)
        if i > 0:
            total_heads = total_heads + zh_in[i]
    out_first[...] = total
    width = hidden_size // (4 * Z_SIZE)
    shift = lax.rem(lanes - width * lax.rem(clip, lanes // width), lanes)
    rolled = pltpu.roll(jnp.concatenate([total_heads] * 4, axis=0), shift, axis=1)
    out_head[...] = rolled[0:2, 0:width]


def store(*refs):
    sem = refs[6]
    copies = [pltpu.make_async_copy(refs[i], refs[3 + i], sem.at[i]) for i in range(3)]
    for copy in copies:
        copy.start()
    for copy in copies:
        copy.wait()


def body(waveform, window_length, first_weight, first_bias, head_weight):
    frame, hidden_size = first_weight.shape[1:]
    hop = frame // 4
    shard = waveform.shape[2] // hop
    frames = shard * 2 * X_SIZE
    count = 2 * frames
    block = (GROUP, hidden_size)
    vmem = pl.BlockSpec(memory_space=pltpu.VMEM)
    hbm = pl.BlockSpec(memory_space=pltpu.HBM)
    coarse, fine = [jnp.asarray(part) for part in twiddles(frame)]
    operands = (waveform[0], coarse, fine, first_weight[0], first_bias, head_weight)
    results = (
        jax.ShapeDtypeStruct((2, shard * hop), F32),
        jax.ShapeDtypeStruct(block, F32),
        jax.ShapeDtypeStruct((2, hidden_size // (4 * Z_SIZE)), F32),
    )
    outs = pl.pallas_call(
        kernel,
        out_shape=results,
        in_specs=[pl.BlockSpec(memory_space=pltpu.SMEM)] + [hbm] * len(operands),
        out_specs=(vmem, vmem, vmem),
        scratch_shapes=[
            pltpu.VMEM((2, shard * hop), BF16),
            pltpu.VMEM((2, shard, hop), F32),
            pltpu.VMEM((2, shard, hop), BF16),
            pltpu.VMEM((1, hidden_size), F32),
            pltpu.VMEM((1, hidden_size), BF16),
            pltpu.VMEM((2 * X_SIZE, 2, shard, hop), BF16),
            pltpu.VMEM(coarse.shape, F32),
            pltpu.VMEM(fine.shape, F32),
            pltpu.VMEM((frame, hidden_size), BF16),
            pltpu.VMEM((frame, frame), BF16),
            pltpu.VMEM((2, frames + 16, hop), F32),
            pltpu.VMEM((count, frame), BF16),
            pltpu.VMEM((count, frame), BF16),
            pltpu.VMEM((count, hidden_size), F32),
            pltpu.VMEM((count, hidden_size), BF16),
            pltpu.VMEM((count, hidden_size), BF16),
            pltpu.VMEM((count, frame), BF16),
            pltpu.VMEM((Z_SIZE, 2, 2) + block, F32),
            pltpu.VMEM((Z_SIZE, 2, 2) + block, BF16),
            pltpu.VMEM((Z_SIZE, 2) + block, BF16),
            pltpu.VMEM((Z_SIZE,) + block, F32),
            pltpu.VMEM((Z_SIZE,) + block, BF16),
            pltpu.VMEM((Z_SIZE,) + block, BF16),
            pltpu.VMEM((Z_SIZE,) + block, BF16),
            pltpu.VMEM((Z_SIZE,) + block, BF16),
            pltpu.VMEM(block, F32),
            pltpu.VMEM((hidden_size // 128, 2, 128), F32),
            pltpu.VMEM((hidden_size // 128, 2, 128), F32),
            pltpu.VMEM((hidden_size // 128, 2, 128), F32),
            pltpu.VMEM((hidden_size // 128, 2, 128), F32),
            pltpu.VMEM((hidden_size // 128, 2, 128), F32),
            pltpu.VMEM((Z_SIZE, 2, 128), F32),
            pltpu.VMEM((2, frames + 16, hop), F32),
            pltpu.VMEM((2, X_SIZE, 2, shard, hop), BF16),
            pltpu.VMEM((3, 2, 2, shard, hop), BF16),
            pltpu.VMEM((2, shard, hop), BF16),
            pltpu.VMEM((2, shard, hop), BF16),
            pltpu.SemaphoreType.DMA((6,)),
            pltpu.SemaphoreType.DMA((7,)),
            pltpu.SemaphoreType.DMA((7,)),
            pltpu.SemaphoreType.DMA((Z_SIZE + 1,)),
            pltpu.SemaphoreType.DMA((Z_SIZE + 1,)),
            pltpu.SemaphoreType.DMA((Z_SIZE + 1,)),
            pltpu.SemaphoreType.DMA((Z_SIZE + 1,)),
            pltpu.SemaphoreType.DMA((Z_SIZE,)),
            pltpu.SemaphoreType.DMA((Z_SIZE,)),
            pltpu.SemaphoreType.DMA((Z_SIZE,)),
            pltpu.SemaphoreType.DMA((Z_SIZE,)),
            pltpu.SemaphoreType.DMA((4,)),
            pltpu.SemaphoreType.DMA((4,)),
            pltpu.SemaphoreType.REGULAR((3,)),
        ],
        compiler_params=pltpu.CompilerParams(
            collective_id=0, has_side_effects=True, vmem_limit_bytes=53000 * 1024
        ),
    )(window_length, *[pltpu.with_memory_space_constraint(part, pltpu.HBM) for part in operands])
    out_wave, out_first, out_head = pl.pallas_call(
        store,
        out_shape=results,
        in_specs=[vmem] * 3,
        out_specs=[hbm] * 3,
        scratch_shapes=[pltpu.SemaphoreType.DMA((3,))],
        compiler_params=pltpu.CompilerParams(vmem_limit_bytes=1024 * 1024),
    )(*outs)
    return out_wave[None], out_first[None], out_head.T[None]


def solution(mesh):
    placed = (
        P("clip", None, "disc"),
        P("disc"),
        P("disc", None, None),
        P("disc", None),
        P("disc", None),
    )
    return jax.shard_map(
        body,
        mesh=mesh,
        in_specs=placed,
        out_specs=(P("clip", None, "disc"), P("disc", "clip", None), P("disc", "clip", None)),
        check_vma=False,
    )
```

```python
import math

import jax
import jax.numpy as jnp
import numpy as np
from jax import lax
from jax.experimental import pallas as pl
from jax.experimental.pallas import tpu as pltpu
from jax.sharding import PartitionSpec as P

GEN_WEIGHT = 10.0
LEAK = 0.2
MESH = pl.DeviceIdType.MESH
GROUP = 16
X_SIZE = 4
Z_SIZE = 16
F32 = jnp.float32
BF16 = jnp.bfloat16


def twiddles(frame):
    column = np.arange(frame // 2)
    coarse = (np.arange(0, frame, GROUP)[:, None] * column[None, :]) % frame
    fine = (np.arange(GROUP)[:, None] * column[None, :]) % frame
    angle = 2.0 * np.pi / frame
    coarse = np.concatenate([np.cos(coarse * angle), np.sin(coarse * angle)], axis=0)
    fine = np.concatenate([np.cos(fine * angle), np.sin(fine * angle)], axis=0)
    return coarse[:, None, :].astype(np.float32), fine.astype(np.float32)


def cosine(angle):
    square = angle * angle
    total = jnp.full_like(square, 1.0 / math.factorial(16))
    for power in range(14, -1, -2):
        total = 1.0 / math.factorial(power) - total * square
    return total


def remote(src, dst, send_sem, recv_sem, device):
    return pltpu.make_async_remote_copy(
        src_ref=src,
        dst_ref=dst,
        send_sem=send_sem,
        recv_sem=recv_sem,
        device_id=device,
        device_id_type=MESH,
    )


def kernel(
    length_ref,
    wave_hbm,
    coarse_hbm,
    fine_hbm,
    weight_hbm,
    bias_hbm,
    head_hbm,
    out_wave,
    out_first,
    out_head,
    raw,
    staged,
    wave,
    bias,
    head,
    gathered,
    coarse,
    fine,
    weight,
    table,
    padded,
    rows,
    spectrum,
    preact,
    disc_delta,
    gen_delta,
    spec_delta,
    grad,
    grad_low,
    core_in,
    kept,
    pair_out,
    pair_in,
    z_out,
    z_in,
    z_own,
    heads,
    heads_mid,
    heads_all,
    core_heads,
    pair_heads,
    zh_in,
    wave_sum,
    wave_low,
    x_in,
    y_out,
    y_in,
    local_sem,
    gather_send,
    gather_recv,
    core_send,
    core_recv,
    pair_send,
    pair_recv,
    z_send,
    z_recv,
    zh_send,
    zh_recv,
    wave_send,
    wave_recv,
    near_sem,
):
    clip = lax.axis_index("clip")
    disc = lax.axis_index("disc")
    core = lax.rem(clip, 2)
    y_lo = lax.rem(clip // 2, 2)
    z = clip // 4
    inner = lax.rem(clip, 4)
    x = lax.rem(disc, X_SIZE)
    y_hi = disc // X_SIZE
    frame, hidden_size = weight.shape
    half = frame // 2
    hop = frame // 4
    frames = padded.shape[1] - 16
    shard = wave.shape[1]
    lanes = 128

    core_peer = {"clip": clip + 1 - 2 * core}
    pair_peer = {"clip": clip + 2 - 4 * y_lo}
    z_near = [
        {"clip": lax.rem(z + away, Z_SIZE) * 4 + inner} for away in (1, 2, Z_SIZE - 1, Z_SIZE - 2)
    ]
    other = lax.rem(disc + X_SIZE, 2 * X_SIZE)
    y_peer = {"disc": other}
    x_at = [lax.rem(x + k, X_SIZE) for k in range(X_SIZE)]
    x_peer = [{"disc": y_hi * X_SIZE + at} for at in x_at]

    local = ((wave_hbm, raw), (coarse_hbm, coarse), (fine_hbm, fine))
    local += ((bias_hbm, bias), (head_hbm, head), (weight_hbm, weight))
    copies = [
        pltpu.make_async_copy(src, dst, local_sem.at[i]) for i, (src, dst) in enumerate(local)
    ]
    barrier = pltpu.get_barrier_semaphore()
    peers = [y_peer, x_peer[2], x_peer[1], x_peer[3], *z_near, pair_peer, core_peer]
    copies[0].start()
    for peer in peers:
        pl.semaphore_signal(barrier, inc=1, device_id=peer, device_id_type=MESH)
    for copy in copies[1:]:
        copy.start()
    copies[0].wait()
    for h in range(shard):
        part = raw[:, h * hop : (h + 1) * hop].astype(F32)
        for ch in range(2):
            staged[ch, h : h + 1, :] = part[ch : ch + 1, :]
    wave[...] = staged[...].astype(BF16)
    gathered[disc] = staged[...].astype(BF16)
    padded[:, 0:8, :] = jnp.zeros((2, 8, hop), F32)
    padded[:, frames + 8 : frames + 16, :] = jnp.zeros((2, 8, hop), F32)
    pl.semaphore_wait(barrier, len(peers))

    def gather_copy(slot, src, at, peer):
        return remote(src, gathered.at[at], gather_send.at[slot], gather_recv.at[slot], peer)

    to_y = gather_copy(0, wave, disc, y_peer)
    to_x = [gather_copy(k, wave, disc, x_peer[k]) for k in (2, 1, 3)]
    for copy in [to_y] + to_x:
        copy.start()

    for copy in copies[1:3]:
        copy.wait()
    length = length_ref[0]
    start = lax.shift_right_arithmetic(frame - length, 1)
    length_float = length.astype(F32)
    groups = frame // GROUP

    def table_rows(g):
        row = pl.multiple_of(g * GROUP, GROUP)
        position = lax.broadcasted_iota(jnp.int32, (GROUP, lanes), 0) + (row - start)
        inside = (position >= 0) & (position < length)
        angle = jnp.pi * position.astype(F32) / length_float - 0.5 * jnp.pi
        root = cosine(angle)
        factor = jnp.where(inside, root * root * (1.0 / math.sqrt(frame)), 0.0)
        for q in range(half // lanes):
            at = slice(q * lanes, (q + 1) * lanes)
            cos_a = coarse[g, :, at]
            sin_a = coarse[groups + g, :, at]
            cos_b = fine[0:GROUP, at]
            sin_b = fine[GROUP : 2 * GROUP, at]
            real = (cos_a * cos_b - sin_a * sin_b) * factor
            imag = -(sin_a * cos_b + cos_a * sin_b) * factor
            table[pl.ds(row, GROUP), at] = real.astype(BF16)
            table[pl.ds(row, GROUP), half + q * lanes : half + (q + 1) * lanes] = imag.astype(BF16)

    def relay(turn):
        for peer in z_near:
            pl.semaphore_signal(near_sem.at[turn], inc=1, device_id=peer, device_id_type=MESH)

    def relay_wait(turn):
        pl.semaphore_wait(near_sem.at[turn], len(z_near))

    relay(0)
    pl.loop(0, groups // 2)(table_rows)
    to_y.wait_recv()
    forward = [gather_copy(3 + k, gathered.at[other], other, x_peer[k]) for k in (2, 1, 3)]
    for copy in forward:
        copy.start()
    pl.loop(groups // 2, groups)(table_rows)
    for copy in to_x + forward:
        copy.wait_recv()
    for j in range(2 * X_SIZE):
        for ch in range(2):
            padded[ch, 8 + shard * j : 8 + shard * (j + 1), :] = gathered[j, ch].astype(F32)
    for piece in range(4):
        for ch in range(2):
            rows[ch * frames : (ch + 1) * frames, piece * hop : (piece + 1) * hop] = padded[
                ch, 6 + piece : 6 + piece + frames, :
            ].astype(BF16)
    for n in range(4):
        at = slice(n * hop, (n + 1) * hop)
        spectrum[:, at] = jnp.dot(rows[...], table[:, at], preferred_element_type=F32).astype(BF16)
    for copy in copies[3:]:
        copy.wait()
    preact[...] = jnp.dot(spectrum[...], weight[...], preferred_element_type=F32)
    head_wide = head[...].astype(F32)
    step = 64

    def delta_rows(i, sums):
        at = pl.ds(pl.multiple_of(i * step, step), step)
        pre = preact[at, :] + bias[...]
        slopes = jnp.where(pre > 0, 1.0, LEAK)
        hidden = (pre * slopes).astype(BF16).astype(F32)
        logits = jnp.sum(hidden * head_wide, axis=1, keepdims=True)
        disc_low = (logits * head_wide * slopes).astype(BF16)
        disc_delta[at, :] = disc_low
        gen_delta[at, :] = (GEN_WEIGHT * (logits - 1.0) * head_wide * slopes).astype(BF16)
        return (
            sums[0] + jnp.sum(logits * hidden, axis=0, keepdims=True),
            sums[1] + jnp.sum(disc_low.astype(F32), axis=0, keepdims=True),
        )

    zero = jnp.zeros((1, hidden_size), F32)
    sums = lax.fori_loop(0, 2 * frames // step, delta_rows, (zero, zero), unroll=2)
    for r in range(hidden_size // lanes):
        for t in range(2):
            heads[r, t : t + 1, :] = sums[t][:, r * lanes : (r + 1) * lanes]

    def core_copy(i):
        return remote(
            grad_low.at[i, :, 1 - core],
            core_in.at[i],
            core_send.at[i],
            core_recv.at[i],
            core_peer,
        )

    def pair_copy(i):
        return remote(pair_out.at[i], pair_in.at[i], pair_send.at[i], pair_recv.at[i], pair_peer)

    core_heads_copy = remote(
        heads, core_heads, core_send.at[Z_SIZE], core_recv.at[Z_SIZE], core_peer
    )
    pair_heads_copy = remote(
        heads_mid, pair_heads, pair_send.at[Z_SIZE], pair_recv.at[Z_SIZE], pair_peer
    )
    core_heads_copy.start()
    for n in range(4):
        at = slice(n * hop, (n + 1) * hop)
        part = lax.dot_general(
            spectrum[:, at], disc_delta[...], (((0,), (0,)), ((), ())), preferred_element_type=F32
        ).reshape(Z_SIZE // 4, 2, 2, GROUP, hidden_size)
        grad[n * 4 : (n + 1) * 4] = part
        grad_low[n * 4 : (n + 1) * 4] = part.astype(BF16)
        if n > 0:
            pl.loop(4 * (n - 1), 4 * n)(lambda i: core_copy(i).start())
    pl.loop(Z_SIZE - 4, Z_SIZE)(lambda i: core_copy(i).start())

    relay_wait(0)
    relay(1)

    spec_delta[...] = lax.dot_general(
        gen_delta[...], weight[...], (((1,), (1,)), ((), ())), preferred_element_type=F32
    ).astype(BF16)
    for piece in (2, 0, 1, 3):
        back = lax.dot_general(
            spec_delta[...],
            table[piece * hop : (piece + 1) * hop, :],
            (((1,), (1,)), ((), ())),
            preferred_element_type=F32,
        ).reshape(2, frames, hop)
        at = slice(6 + piece, 6 + piece + frames)
        if piece == 2:
            wave_sum[:, at, :] = back
        else:
            wave_sum[:, at, :] = wave_sum[:, at, :] + back

    relay_wait(1)
    relay(2)

    core_heads_copy.wait_recv()
    heads_mid[...] = heads[...] + core_heads[...]
    pair_heads_copy.start()

    @pl.loop(0, Z_SIZE)
    def _(i):
        core_copy(i).wait_recv()
        pair_out[i] = (grad[i, 1 - y_lo, core] + core_in[i, 1 - y_lo].astype(F32)).astype(BF16)
        pair_copy(i).start()
        kept[i] = grad[i, y_lo, core] + core_in[i, y_lo].astype(F32)

    for j in range(2 * X_SIZE):
        for ch in range(2):
            wave_low[j // X_SIZE, j % X_SIZE, ch] = wave_sum[
                ch, 8 + shard * j : 8 + shard * (j + 1), :
            ].astype(BF16)

    def x_copy(k):
        return remote(
            wave_low.at[:, x_at[k]],
            x_in.at[k - 1],
            wave_send.at[k - 1],
            wave_recv.at[k - 1],
            x_peer[k],
        )

    y_copy = remote(y_out, y_in, wave_send.at[3], wave_recv.at[3], y_peer)
    for k in (2, 1, 3):
        x_copy(k).start()

    pair_heads_copy.wait_recv()
    heads_all[...] = heads_mid[...] + pair_heads[...]
    relay_wait(2)

    def z_copy(to, slot):
        peer = {"clip": to * 4 + inner}
        return remote(z_out.at[to], z_in.at[slot], z_send.at[to], z_recv.at[slot], peer)

    def zh_copy(to, slot):
        peer = {"clip": to * 4 + inner}
        return remote(heads_all.at[to // 4], zh_in.at[slot], zh_send.at[to], zh_recv.at[slot], peer)

    @pl.loop(0, Z_SIZE)
    def _(i):
        pair_copy(i).wait_recv()
        total = kept[i] + pair_in[i].astype(F32)

        @pl.when(i != z)
        def _():
            z_out[i] = total.astype(BF16)
            z_copy(i, z).start()
            zh_copy(i, z).start()

        @pl.when(i == z)
        def _():
            z_own[...] = total

    for k in (2, 1, 3):
        x_copy(k).wait_recv()

    def x_sum(at):
        total = wave_low[at, x].astype(F32)
        for k in range(3):
            total = total + x_in[k, at].astype(F32)
        return total

    y_out[...] = x_sum(1 - y_hi).astype(BF16)
    y_copy.start()
    staged[...] = x_sum(y_hi)
    z_in[z] = jnp.zeros((GROUP, hidden_size), BF16)
    zh_in[z] = heads_all[z // 4]
    y_copy.wait_recv()
    staged[...] = staged[...] + y_in[...].astype(F32)
    for h in range(shard):
        for ch in range(2):
            out_wave[ch : ch + 1, h * hop : (h + 1) * hop] = staged[ch, h : h + 1, :]

    for copy in [to_y] + to_x + forward:
        copy.wait_send()
    core_heads_copy.wait_send()
    pair_heads_copy.wait_send()

    @pl.loop(0, Z_SIZE)
    def _(i):
        core_copy(i).wait_send()
        pair_copy(i).wait_send()

    @pl.loop(0, Z_SIZE)
    def _(i):
        @pl.when(i != z)
        def _():
            z_copy(i, z).wait_send()
            zh_copy(i, z).wait_send()

    for k in (2, 1, 3):
        x_copy(k).wait_send()
    y_copy.wait_send()

    @pl.loop(0, Z_SIZE)
    def _(i):
        @pl.when(i != z)
        def _():
            z_copy(i, i).wait_recv()
            zh_copy(i, i).wait_recv()

    total = z_own[...]
    total_heads = zh_in[0]
    for i in range(Z_SIZE):
        total = total + z_in[i].astype(F32)
        if i > 0:
            total_heads = total_heads + zh_in[i]
    out_first[...] = total
    width = hidden_size // (4 * Z_SIZE)
    shift = lax.rem(lanes - width * lax.rem(clip, lanes // width), lanes)
    rolled = pltpu.roll(jnp.concatenate([total_heads] * 4, axis=0), shift, axis=1)
    out_head[...] = rolled[0:2, 0:width]


def store(*refs):
    sem = refs[6]
    copies = [pltpu.make_async_copy(refs[i], refs[3 + i], sem.at[i]) for i in range(3)]
    for copy in copies:
        copy.start()
    for copy in copies:
        copy.wait()


def body(waveform, window_length, first_weight, first_bias, head_weight):
    frame, hidden_size = first_weight.shape[1:]
    hop = frame // 4
    shard = waveform.shape[2] // hop
    frames = shard * 2 * X_SIZE
    count = 2 * frames
    block = (GROUP, hidden_size)
    vmem = pl.BlockSpec(memory_space=pltpu.VMEM)
    hbm = pl.BlockSpec(memory_space=pltpu.HBM)
    coarse, fine = [jnp.asarray(part) for part in twiddles(frame)]
    operands = (waveform[0], coarse, fine, first_weight[0], first_bias, head_weight)
    results = (
        jax.ShapeDtypeStruct((2, shard * hop), F32),
        jax.ShapeDtypeStruct(block, F32),
        jax.ShapeDtypeStruct((2, hidden_size // (4 * Z_SIZE)), F32),
    )
    outs = pl.pallas_call(
        kernel,
        out_shape=results,
        in_specs=[pl.BlockSpec(memory_space=pltpu.SMEM)] + [hbm] * len(operands),
        out_specs=(vmem, vmem, vmem),
        scratch_shapes=[
            pltpu.VMEM((2, shard * hop), BF16),
            pltpu.VMEM((2, shard, hop), F32),
            pltpu.VMEM((2, shard, hop), BF16),
            pltpu.VMEM((1, hidden_size), F32),
            pltpu.VMEM((1, hidden_size), BF16),
            pltpu.VMEM((2 * X_SIZE, 2, shard, hop), BF16),
            pltpu.VMEM(coarse.shape, F32),
            pltpu.VMEM(fine.shape, F32),
            pltpu.VMEM((frame, hidden_size), BF16),
            pltpu.VMEM((frame, frame), BF16),
            pltpu.VMEM((2, frames + 16, hop), F32),
            pltpu.VMEM((count, frame), BF16),
            pltpu.VMEM((count, frame), BF16),
            pltpu.VMEM((count, hidden_size), F32),
            pltpu.VMEM((count, hidden_size), BF16),
            pltpu.VMEM((count, hidden_size), BF16),
            pltpu.VMEM((count, frame), BF16),
            pltpu.VMEM((Z_SIZE, 2, 2) + block, F32),
            pltpu.VMEM((Z_SIZE, 2, 2) + block, BF16),
            pltpu.VMEM((Z_SIZE, 2) + block, BF16),
            pltpu.VMEM((Z_SIZE,) + block, F32),
            pltpu.VMEM((Z_SIZE,) + block, BF16),
            pltpu.VMEM((Z_SIZE,) + block, BF16),
            pltpu.VMEM((Z_SIZE,) + block, BF16),
            pltpu.VMEM((Z_SIZE,) + block, BF16),
            pltpu.VMEM(block, F32),
            pltpu.VMEM((hidden_size // 128, 2, 128), F32),
            pltpu.VMEM((hidden_size // 128, 2, 128), F32),
            pltpu.VMEM((hidden_size // 128, 2, 128), F32),
            pltpu.VMEM((hidden_size // 128, 2, 128), F32),
            pltpu.VMEM((hidden_size // 128, 2, 128), F32),
            pltpu.VMEM((Z_SIZE, 2, 128), F32),
            pltpu.VMEM((2, frames + 16, hop), F32),
            pltpu.VMEM((2, X_SIZE, 2, shard, hop), BF16),
            pltpu.VMEM((3, 2, 2, shard, hop), BF16),
            pltpu.VMEM((2, shard, hop), BF16),
            pltpu.VMEM((2, shard, hop), BF16),
            pltpu.SemaphoreType.DMA((6,)),
            pltpu.SemaphoreType.DMA((7,)),
            pltpu.SemaphoreType.DMA((7,)),
            pltpu.SemaphoreType.DMA((Z_SIZE + 1,)),
            pltpu.SemaphoreType.DMA((Z_SIZE + 1,)),
            pltpu.SemaphoreType.DMA((Z_SIZE + 1,)),
            pltpu.SemaphoreType.DMA((Z_SIZE + 1,)),
            pltpu.SemaphoreType.DMA((Z_SIZE,)),
            pltpu.SemaphoreType.DMA((Z_SIZE,)),
            pltpu.SemaphoreType.DMA((Z_SIZE,)),
            pltpu.SemaphoreType.DMA((Z_SIZE,)),
            pltpu.SemaphoreType.DMA((4,)),
            pltpu.SemaphoreType.DMA((4,)),
            pltpu.SemaphoreType.REGULAR((3,)),
        ],
        compiler_params=pltpu.CompilerParams(
            collective_id=0, has_side_effects=True, vmem_limit_bytes=53000 * 1024
        ),
    )(window_length, *[pltpu.with_memory_space_constraint(part, pltpu.HBM) for part in operands])
    out_wave, out_first, out_head = pl.pallas_call(
        store,
        out_shape=results,
        in_specs=[vmem] * 3,
        out_specs=[hbm] * 3,
        scratch_shapes=[pltpu.SemaphoreType.DMA((3,))],
        compiler_params=pltpu.CompilerParams(vmem_limit_bytes=1024 * 1024),
    )(*outs)
    return out_wave[None], out_first[None], out_head.T[None]


def solution(mesh):
    placed = (
        P("clip", None, "disc"),
        P("disc"),
        P("disc", None, None),
        P("disc", None),
        P("disc", None),
    )
    return jax.shard_map(
        body,
        mesh=mesh,
        in_specs=placed,
        out_specs=(P("clip", None, "disc"), P("disc", "clip", None), P("disc", "clip", None)),
        check_vma=False,
    )
```

```python
import math

import jax
import jax.numpy as jnp
import numpy as np
from jax import lax
from jax.experimental import pallas as pl
from jax.experimental.pallas import tpu as pltpu
from jax.sharding import PartitionSpec as P

GEN_WEIGHT = 10.0
LEAK = 0.2
MESH = pl.DeviceIdType.MESH
GROUP = 16
X_SIZE = 4
Z_SIZE = 16
F32 = jnp.float32
BF16 = jnp.bfloat16


def twiddles(frame):
    column = np.arange(frame // 2)
    coarse = (np.arange(0, frame, GROUP)[:, None] * column[None, :]) % frame
    fine = (np.arange(GROUP)[:, None] * column[None, :]) % frame
    angle = 2.0 * np.pi / frame
    coarse = np.concatenate([np.cos(coarse * angle), np.sin(coarse * angle)], axis=0)
    fine = np.concatenate([np.cos(fine * angle), np.sin(fine * angle)], axis=0)
    return coarse[:, None, :].astype(np.float32), fine.astype(np.float32)


def cosine(angle):
    square = angle * angle
    total = jnp.full_like(square, 1.0 / math.factorial(16))
    for power in range(14, -1, -2):
        total = 1.0 / math.factorial(power) - total * square
    return total


def remote(src, dst, send_sem, recv_sem, device):
    return pltpu.make_async_remote_copy(
        src_ref=src,
        dst_ref=dst,
        send_sem=send_sem,
        recv_sem=recv_sem,
        device_id=device,
        device_id_type=MESH,
    )


def kernel(
    length_ref,
    wave_hbm,
    coarse_hbm,
    fine_hbm,
    weight_hbm,
    bias_hbm,
    head_hbm,
    out_wave,
    out_first,
    out_head,
    raw,
    staged,
    wave,
    bias,
    head,
    gathered,
    coarse,
    fine,
    weight,
    table,
    padded,
    rows,
    spectrum,
    preact,
    disc_delta,
    gen_delta,
    spec_delta,
    grad,
    grad_low,
    core_in,
    kept,
    pair_out,
    pair_in,
    z_out,
    z_in,
    z_own,
    heads,
    heads_mid,
    heads_all,
    core_heads,
    pair_heads,
    zh_in,
    wave_sum,
    wave_low,
    x_in,
    y_out,
    y_in,
    local_sem,
    gather_send,
    gather_recv,
    core_send,
    core_recv,
    pair_send,
    pair_recv,
    z_send,
    z_recv,
    zh_send,
    zh_recv,
    wave_send,
    wave_recv,
    near_sem,
):
    clip = lax.axis_index("clip")
    disc = lax.axis_index("disc")
    core = lax.rem(clip, 2)
    y_lo = lax.rem(clip // 2, 2)
    z = clip // 4
    inner = lax.rem(clip, 4)
    x = lax.rem(disc, X_SIZE)
    y_hi = disc // X_SIZE
    frame, hidden_size = weight.shape
    half = frame // 2
    hop = frame // 4
    frames = padded.shape[1] - 16
    shard = wave.shape[1]
    lanes = 128

    core_peer = {"clip": clip + 1 - 2 * core}
    pair_peer = {"clip": clip + 2 - 4 * y_lo}
    z_near = [
        {"clip": lax.rem(z + away, Z_SIZE) * 4 + inner} for away in (1, 2, Z_SIZE - 1, Z_SIZE - 2)
    ]
    other = lax.rem(disc + X_SIZE, 2 * X_SIZE)
    y_peer = {"disc": other}
    x_at = [lax.rem(x + k, X_SIZE) for k in range(X_SIZE)]
    x_peer = [{"disc": y_hi * X_SIZE + at} for at in x_at]

    local = ((wave_hbm, raw), (coarse_hbm, coarse), (fine_hbm, fine))
    local += ((bias_hbm, bias), (head_hbm, head), (weight_hbm, weight))
    copies = [
        pltpu.make_async_copy(src, dst, local_sem.at[i]) for i, (src, dst) in enumerate(local)
    ]
    barrier = pltpu.get_barrier_semaphore()
    peers = [y_peer, x_peer[2], x_peer[1], x_peer[3], *z_near, pair_peer, core_peer]
    copies[0].start()
    for peer in peers:
        pl.semaphore_signal(barrier, inc=1, device_id=peer, device_id_type=MESH)
    for copy in copies[1:]:
        copy.start()
    copies[0].wait()
    for h in range(shard):
        part = raw[:, h * hop : (h + 1) * hop].astype(F32)
        for ch in range(2):
            staged[ch, h : h + 1, :] = part[ch : ch + 1, :]
    wave[...] = staged[...].astype(BF16)
    gathered[disc] = staged[...].astype(BF16)
    padded[:, 0:8, :] = jnp.zeros((2, 8, hop), F32)
    padded[:, frames + 8 : frames + 16, :] = jnp.zeros((2, 8, hop), F32)
    pl.semaphore_wait(barrier, len(peers))

    def gather_copy(slot, src, at, peer):
        return remote(src, gathered.at[at], gather_send.at[slot], gather_recv.at[slot], peer)

    to_y = gather_copy(0, wave, disc, y_peer)
    to_x = [gather_copy(k, wave, disc, x_peer[k]) for k in (2, 1, 3)]
    for copy in [to_y] + to_x:
        copy.start()

    for copy in copies[1:3]:
        copy.wait()
    length = length_ref[0]
    start = lax.shift_right_arithmetic(frame - length, 1)
    length_float = length.astype(F32)
    groups = frame // GROUP

    def table_rows(g):
        row = pl.multiple_of(g * GROUP, GROUP)
        position = lax.broadcasted_iota(jnp.int32, (GROUP, lanes), 0) + (row - start)
        inside = (position >= 0) & (position < length)
        angle = jnp.pi * position.astype(F32) / length_float - 0.5 * jnp.pi
        root = cosine(angle)
        factor = jnp.where(inside, root * root * (1.0 / math.sqrt(frame)), 0.0)
        for q in range(half // lanes):
            at = slice(q * lanes, (q + 1) * lanes)
            cos_a = coarse[g, :, at]
            sin_a = coarse[groups + g, :, at]
            cos_b = fine[0:GROUP, at]
            sin_b = fine[GROUP : 2 * GROUP, at]
            real = (cos_a * cos_b - sin_a * sin_b) * factor
            imag = -(sin_a * cos_b + cos_a * sin_b) * factor
            table[pl.ds(row, GROUP), at] = real.astype(BF16)
            table[pl.ds(row, GROUP), half + q * lanes : half + (q + 1) * lanes] = imag.astype(BF16)

    def relay(turn):
        for peer in z_near:
            pl.semaphore_signal(near_sem.at[turn], inc=1, device_id=peer, device_id_type=MESH)

    def relay_wait(turn):
        pl.semaphore_wait(near_sem.at[turn], len(z_near))

    relay(0)
    pl.loop(0, groups // 2)(table_rows)
    to_y.wait_recv()
    forward = [gather_copy(3 + k, gathered.at[other], other, x_peer[k]) for k in (2, 1, 3)]
    for copy in forward:
        copy.start()
    pl.loop(groups // 2, groups)(table_rows)
    for copy in to_x + forward:
        copy.wait_recv()
    for j in range(2 * X_SIZE):
        for ch in range(2):
            padded[ch, 8 + shard * j : 8 + shard * (j + 1), :] = gathered[j, ch].astype(F32)
    for piece in range(4):
        for ch in range(2):
            rows[ch * frames : (ch + 1) * frames, piece * hop : (piece + 1) * hop] = padded[
                ch, 6 + piece : 6 + piece + frames, :
            ].astype(BF16)
    for n in range(4):
        at = slice(n * hop, (n + 1) * hop)
        spectrum[:, at] = jnp.dot(rows[...], table[:, at], preferred_element_type=F32).astype(BF16)
    for copy in copies[3:]:
        copy.wait()
    preact[...] = jnp.dot(spectrum[...], weight[...], preferred_element_type=F32)
    head_wide = head[...].astype(F32)
    step = 64

    def delta_rows(i, sums):
        at = pl.ds(pl.multiple_of(i * step, step), step)
        pre = preact[at, :] + bias[...]
        slopes = jnp.where(pre > 0, 1.0, LEAK)
        hidden = (pre * slopes).astype(BF16).astype(F32)
        logits = jnp.sum(hidden * head_wide, axis=1, keepdims=True)
        disc_low = (logits * head_wide * slopes).astype(BF16)
        disc_delta[at, :] = disc_low
        gen_delta[at, :] = (GEN_WEIGHT * (logits - 1.0) * head_wide * slopes).astype(BF16)
        return (
            sums[0] + jnp.sum(logits * hidden, axis=0, keepdims=True),
            sums[1] + jnp.sum(disc_low.astype(F32), axis=0, keepdims=True),
        )

    zero = jnp.zeros((1, hidden_size), F32)
    sums = lax.fori_loop(0, 2 * frames // step, delta_rows, (zero, zero), unroll=4)
    for r in range(hidden_size // lanes):
        for t in range(2):
            heads[r, t : t + 1, :] = sums[t][:, r * lanes : (r + 1) * lanes]

    def core_copy(i):
        return remote(
            grad_low.at[i, :, 1 - core],
            core_in.at[i],
            core_send.at[i],
            core_recv.at[i],
            core_peer,
        )

    def pair_copy(i):
        return remote(pair_out.at[i], pair_in.at[i], pair_send.at[i], pair_recv.at[i], pair_peer)

    core_heads_copy = remote(
        heads, core_heads, core_send.at[Z_SIZE], core_recv.at[Z_SIZE], core_peer
    )
    pair_heads_copy = remote(
        heads_mid, pair_heads, pair_send.at[Z_SIZE], pair_recv.at[Z_SIZE], pair_peer
    )
    core_heads_copy.start()
    for n in range(4):
        at = slice(n * hop, (n + 1) * hop)
        part = lax.dot_general(
            spectrum[:, at], disc_delta[...], (((0,), (0,)), ((), ())), preferred_element_type=F32
        ).reshape(Z_SIZE // 4, 2, 2, GROUP, hidden_size)
        grad[n * 4 : (n + 1) * 4] = part
        grad_low[n * 4 : (n + 1) * 4] = part.astype(BF16)
        if n > 0:
            pl.loop(4 * (n - 1), 4 * n)(lambda i: core_copy(i).start())
    pl.loop(Z_SIZE - 4, Z_SIZE)(lambda i: core_copy(i).start())

    relay_wait(0)
    relay(1)

    spec_delta[...] = lax.dot_general(
        gen_delta[...], weight[...], (((1,), (1,)), ((), ())), preferred_element_type=F32
    ).astype(BF16)
    for piece in (2, 0, 1, 3):
        back = lax.dot_general(
            spec_delta[...],
            table[piece * hop : (piece + 1) * hop, :],
            (((1,), (1,)), ((), ())),
            preferred_element_type=F32,
        ).reshape(2, frames, hop)
        at = slice(6 + piece, 6 + piece + frames)
        if piece == 2:
            wave_sum[:, at, :] = back
        else:
            wave_sum[:, at, :] = wave_sum[:, at, :] + back

    relay_wait(1)
    relay(2)

    core_heads_copy.wait_recv()
    heads_mid[...] = heads[...] + core_heads[...]
    pair_heads_copy.start()

    @pl.loop(0, Z_SIZE, unroll=2)
    def _(i):
        core_copy(i).wait_recv()
        pair_out[i] = (grad[i, 1 - y_lo, core] + core_in[i, 1 - y_lo].astype(F32)).astype(BF16)
        pair_copy(i).start()
        kept[i] = grad[i, y_lo, core] + core_in[i, y_lo].astype(F32)

    for j in range(2 * X_SIZE):
        for ch in range(2):
            wave_low[j // X_SIZE, j % X_SIZE, ch] = wave_sum[
                ch, 8 + shard * j : 8 + shard * (j + 1), :
            ].astype(BF16)

    def x_copy(k):
        return remote(
            wave_low.at[:, x_at[k]],
            x_in.at[k - 1],
            wave_send.at[k - 1],
            wave_recv.at[k - 1],
            x_peer[k],
        )

    y_copy = remote(y_out, y_in, wave_send.at[3], wave_recv.at[3], y_peer)
    for k in (2, 1, 3):
        x_copy(k).start()

    pair_heads_copy.wait_recv()
    heads_all[...] = heads_mid[...] + pair_heads[...]
    relay_wait(2)

    def z_copy(to, slot):
        peer = {"clip": to * 4 + inner}
        return remote(z_out.at[to], z_in.at[slot], z_send.at[to], z_recv.at[slot], peer)

    def zh_copy(to, slot):
        peer = {"clip": to * 4 + inner}
        return remote(heads_all.at[to // 4], zh_in.at[slot], zh_send.at[to], zh_recv.at[slot], peer)

    @pl.loop(0, Z_SIZE)
    def _(i):
        pair_copy(i).wait_recv()
        total = kept[i] + pair_in[i].astype(F32)

        @pl.when(i != z)
        def _():
            z_out[i] = total.astype(BF16)
            z_copy(i, z).start()
            zh_copy(i, z).start()

        @pl.when(i == z)
        def _():
            z_own[...] = total

    for k in (2, 1, 3):
        x_copy(k).wait_recv()

    def x_sum(at):
        total = wave_low[at, x].astype(F32)
        for k in range(3):
            total = total + x_in[k, at].astype(F32)
        return total

    y_out[...] = x_sum(1 - y_hi).astype(BF16)
    y_copy.start()
    staged[...] = x_sum(y_hi)
    z_in[z] = jnp.zeros((GROUP, hidden_size), BF16)
    zh_in[z] = heads_all[z // 4]
    y_copy.wait_recv()
    staged[...] = staged[...] + y_in[...].astype(F32)
    for h in range(shard):
        for ch in range(2):
            out_wave[ch : ch + 1, h * hop : (h + 1) * hop] = staged[ch, h : h + 1, :]

    for copy in [to_y] + to_x + forward:
        copy.wait_send()
    core_heads_copy.wait_send()
    pair_heads_copy.wait_send()

    @pl.loop(0, Z_SIZE)
    def _(i):
        core_copy(i).wait_send()
        pair_copy(i).wait_send()

    @pl.loop(0, Z_SIZE)
    def _(i):
        @pl.when(i != z)
        def _():
            z_copy(i, z).wait_send()
            zh_copy(i, z).wait_send()

    for k in (2, 1, 3):
        x_copy(k).wait_send()
    y_copy.wait_send()

    @pl.loop(0, Z_SIZE)
    def _(i):
        @pl.when(i != z)
        def _():
            z_copy(i, i).wait_recv()
            zh_copy(i, i).wait_recv()

    total = z_own[...]
    total_heads = zh_in[0]
    for i in range(Z_SIZE):
        total = total + z_in[i].astype(F32)
        if i > 0:
            total_heads = total_heads + zh_in[i]
    out_first[...] = total
    width = hidden_size // (4 * Z_SIZE)
    shift = lax.rem(lanes - width * lax.rem(clip, lanes // width), lanes)
    rolled = pltpu.roll(jnp.concatenate([total_heads] * 4, axis=0), shift, axis=1)
    out_head[...] = rolled[0:2, 0:width]


def store(*refs):
    sem = refs[6]
    copies = [pltpu.make_async_copy(refs[i], refs[3 + i], sem.at[i]) for i in range(3)]
    for copy in copies:
        copy.start()
    for copy in copies:
        copy.wait()


def body(waveform, window_length, first_weight, first_bias, head_weight):
    frame, hidden_size = first_weight.shape[1:]
    hop = frame // 4
    shard = waveform.shape[2] // hop
    frames = shard * 2 * X_SIZE
    count = 2 * frames
    block = (GROUP, hidden_size)
    vmem = pl.BlockSpec(memory_space=pltpu.VMEM)
    hbm = pl.BlockSpec(memory_space=pltpu.HBM)
    coarse, fine = [jnp.asarray(part) for part in twiddles(frame)]
    operands = (waveform[0], coarse, fine, first_weight[0], first_bias, head_weight)
    results = (
        jax.ShapeDtypeStruct((2, shard * hop), F32),
        jax.ShapeDtypeStruct(block, F32),
        jax.ShapeDtypeStruct((2, hidden_size // (4 * Z_SIZE)), F32),
    )
    outs = pl.pallas_call(
        kernel,
        out_shape=results,
        in_specs=[pl.BlockSpec(memory_space=pltpu.SMEM)] + [hbm] * len(operands),
        out_specs=(vmem, vmem, vmem),
        scratch_shapes=[
            pltpu.VMEM((2, shard * hop), BF16),
            pltpu.VMEM((2, shard, hop), F32),
            pltpu.VMEM((2, shard, hop), BF16),
            pltpu.VMEM((1, hidden_size), F32),
            pltpu.VMEM((1, hidden_size), BF16),
            pltpu.VMEM((2 * X_SIZE, 2, shard, hop), BF16),
            pltpu.VMEM(coarse.shape, F32),
            pltpu.VMEM(fine.shape, F32),
            pltpu.VMEM((frame, hidden_size), BF16),
            pltpu.VMEM((frame, frame), BF16),
            pltpu.VMEM((2, frames + 16, hop), F32),
            pltpu.VMEM((count, frame), BF16),
            pltpu.VMEM((count, frame), BF16),
            pltpu.VMEM((count, hidden_size), F32),
            pltpu.VMEM((count, hidden_size), BF16),
            pltpu.VMEM((count, hidden_size), BF16),
            pltpu.VMEM((count, frame), BF16),
            pltpu.VMEM((Z_SIZE, 2, 2) + block, F32),
            pltpu.VMEM((Z_SIZE, 2, 2) + block, BF16),
            pltpu.VMEM((Z_SIZE, 2) + block, BF16),
            pltpu.VMEM((Z_SIZE,) + block, F32),
            pltpu.VMEM((Z_SIZE,) + block, BF16),
            pltpu.VMEM((Z_SIZE,) + block, BF16),
            pltpu.VMEM((Z_SIZE,) + block, BF16),
            pltpu.VMEM((Z_SIZE,) + block, BF16),
            pltpu.VMEM(block, F32),
            pltpu.VMEM((hidden_size // 128, 2, 128), F32),
            pltpu.VMEM((hidden_size // 128, 2, 128), F32),
            pltpu.VMEM((hidden_size // 128, 2, 128), F32),
            pltpu.VMEM((hidden_size // 128, 2, 128), F32),
            pltpu.VMEM((hidden_size // 128, 2, 128), F32),
            pltpu.VMEM((Z_SIZE, 2, 128), F32),
            pltpu.VMEM((2, frames + 16, hop), F32),
            pltpu.VMEM((2, X_SIZE, 2, shard, hop), BF16),
            pltpu.VMEM((3, 2, 2, shard, hop), BF16),
            pltpu.VMEM((2, shard, hop), BF16),
            pltpu.VMEM((2, shard, hop), BF16),
            pltpu.SemaphoreType.DMA((6,)),
            pltpu.SemaphoreType.DMA((7,)),
            pltpu.SemaphoreType.DMA((7,)),
            pltpu.SemaphoreType.DMA((Z_SIZE + 1,)),
            pltpu.SemaphoreType.DMA((Z_SIZE + 1,)),
            pltpu.SemaphoreType.DMA((Z_SIZE + 1,)),
            pltpu.SemaphoreType.DMA((Z_SIZE + 1,)),
            pltpu.SemaphoreType.DMA((Z_SIZE,)),
            pltpu.SemaphoreType.DMA((Z_SIZE,)),
            pltpu.SemaphoreType.DMA((Z_SIZE,)),
            pltpu.SemaphoreType.DMA((Z_SIZE,)),
            pltpu.SemaphoreType.DMA((4,)),
            pltpu.SemaphoreType.DMA((4,)),
            pltpu.SemaphoreType.REGULAR((3,)),
        ],
        compiler_params=pltpu.CompilerParams(
            collective_id=0, has_side_effects=True, vmem_limit_bytes=53000 * 1024
        ),
    )(window_length, *[pltpu.with_memory_space_constraint(part, pltpu.HBM) for part in operands])
    out_wave, out_first, out_head = pl.pallas_call(
        store,
        out_shape=results,
        in_specs=[vmem] * 3,
        out_specs=[hbm] * 3,
        scratch_shapes=[pltpu.SemaphoreType.DMA((3,))],
        compiler_params=pltpu.CompilerParams(vmem_limit_bytes=1024 * 1024),
    )(*outs)
    return out_wave[None], out_first[None], out_head.T[None]


def solution(mesh):
    placed = (
        P("clip", None, "disc"),
        P("disc"),
        P("disc", None, None),
        P("disc", None),
        P("disc", None),
    )
    return jax.shard_map(
        body,
        mesh=mesh,
        in_specs=placed,
        out_specs=(P("clip", None, "disc"), P("disc", "clip", None), P("disc", "clip", None)),
        check_vma=False,
    )
```
